128 devices in a mesh: ctx: 128 (over z, y, x, core).
Axes of the slice: x: 4, y: 4, z: 4, core: 2. Of those that a mesh axis runs over, the one named last changes fastest.
Arguments:
- normed_input: bfloat16 [32768, 5120], P('ctx'), may hold values from -6 to 6
- frozen_query_output: bfloat16 [32768, 5120], P('ctx'), may hold values from -6 to 6
- key_base: bfloat16 [32768, 1024], P('ctx'), may hold values from -6 to 6
- frozen_value_output: bfloat16 [32768, 1024], P('ctx'), may hold values from -6 to 6
- out_grad: bfloat16 [32768, 5120], P('ctx'), may hold values from -6 to 6
- query_down_factor: bfloat16 [5120, 64], replicated, may hold values from -0.078125 to 0.078125
- query_up_factor: bfloat16 [64, 5120], replicated, may hold values from -0.375 to 0.375
- value_down_factor: bfloat16 [5120, 64], replicated, may hold values from -0.078125 to 0.078125
- value_up_factor: bfloat16 [64, 1024], replicated, may hold values from -0.375 to 0.375
- doc_lengths: int32 [64], replicated, may hold values from 1 to 1024, 32768 in all
- stretch_map: int32 [128], replicated, may hold values from 0 to 127, as said below
Outputs:
- attended: bfloat16 [32768, 5120], P('ctx')
- key_grad: bfloat16 [32768, 1024], P('ctx')
- grad_down_q: float32 [5120, 64], replicated
- query_up_gradient: float32 [64, 5120], replicated
- grad_down_v: float32 [5120, 64], replicated
- value_up_gradient: float32 [64, 1024], replicated
The draws below stay inside these ranges and needn't reach their ends.
Inputs may be any that keep to these rules, and one draw needn't show every extreme that they name: stretch_map is a permutation in which entry i is i or i with its lowest bit flipped; entries 0 and 1, and entries 128 / 2 and 65, are always flipped. `doc_lengths`: the lengths sum to 32768 and the longest is exactly 1024.
All inputs are finite; a program needn't handle non-finite values.
Results may differ from the reference program's by a relative error of at most 0.013.
The reference program's roundings to bfloat16 on the way count: a program that leaves them out, or rounds other values in their place, can miss the bound.
Values may be sent and summed in bfloat16 or wider, within the bound.
No kernel may reach another device: no remote copies, remote signals or barrier semaphores. Data moves between devices by JAX's collectives and lax.ppermute only.
A program may use at most 192 MiB of HBM per device.

```python
import math
import jax
import jax.numpy as jnp
import numpy as np
from jax import lax

D = 5120
H = 40
KVH = 8
HD = 128
R = 64
TOK_DEV = 256
STRETCHES = 128
TOKEN_COUNT = 32768
MOST = 1024
NDOC = 64


def background(key, shape):
    return jnp.clip(jax.random.normal(key, shape), -5.0, 5.0)


def draw_frozen_query_output(key, part):
    base = background(jax.random.fold_in(key, 1), (TOKEN_COUNT, H, HD))
    return base.reshape(TOKEN_COUNT, H * HD).astype(jnp.bfloat16)


def draw_key_base(key, part):
    base = background(jax.random.fold_in(key, 2), (TOKEN_COUNT, KVH, HD))
    return base.reshape(TOKEN_COUNT, KVH * HD).astype(jnp.bfloat16)


def draw_stretch_map(key, part):
    flags = jax.random.randint(key, (STRETCHES // 2,), 0, 2).astype(jnp.int32)
    flags = flags.at[0].set(1).at[STRETCHES // 4].set(1)
    indices = jnp.arange(STRETCHES, dtype=jnp.int32)
    return jnp.bitwise_xor(indices, flags[indices // 2]).astype(jnp.int32)


def block_scale(rng, shape, pieces, least, high):
    level, own = 1.0, jax.random.fold_in(rng, 6)
    for axis_at, parts in pieces:
        heights = jnp.exp(jax.random.uniform(jax.random.fold_in(own, axis_at), (parts,), jnp.float32, least / len(pieces), high / len(pieces)))
        level = level * jnp.repeat(heights, shape[axis_at] // parts).reshape([-1 if axis == axis_at else 1 for axis in range(len(shape))])
    return level


def profile(count, total, reach, skew):
    weights = [(1 << 20) // math.isqrt(standing ** skew) + 1 for standing in range(2, count + 1)]
    spare, counts = total - reach - (count - 1), [1] * (count - 1)
    while spare > 0:
        candidates = [i for i in range(count - 1) if counts[i] < reach]
        whole, left = sum([weights[i] for i in candidates]), spare
        for i in candidates:
            addition = min(reach - counts[i], max(1, left * weights[i] // whole), spare)
            counts[i] = counts[i] + addition
            spare = spare - addition
    return np.array([reach] + counts)


def ragged_sizes(stream_key, amount, total, bound, slope):
    if amount == 2:
        one = jax.random.randint(stream_key, (), max(1, total - bound), min(bound, total - 1) + 1)
        return jnp.stack([one, total - one])
    sizes = jnp.asarray(profile(amount, total, bound, slope), jnp.int32)
    twos = (amount - 1) // 2
    giver, taker = sizes[1:1 + 2 * twos:2], sizes[2:2 + 2 * twos:2]
    margin = jnp.minimum(giver - 1, bound - taker)
    moved = jax.random.randint(jax.random.fold_in(stream_key, 1), (twos,), 0, 1 << 20) % (margin + 1)
    sizes = sizes.at[1:1 + 2 * twos:2].set(giver - moved).at[2:2 + 2 * twos:2].set(taker + moved)
    return sizes[jax.random.permutation(jax.random.fold_in(stream_key, 2), amount)]


def normal_values(rng, shape, spread, limit, split=(), kind=jnp.bfloat16):
    drawn = jax.random.normal(rng, shape, jnp.float32) * spread
    if len(split) > 0:
        drawn = block_scale(rng, shape, split, -0.22, 0.18) * drawn
    return jnp.clip(drawn, min=-limit, max=limit).astype(kind)


def setup_inputs(seed: int = 0) -> dict:
    arg_keys = jax.random.split(jax.random.key(seed), 12)
    normed_input = normal_values(arg_keys[0], (TOKEN_COUNT, D), 1.0, 6.0, ((0, 128),))
    frozen_query_output = draw_frozen_query_output(jax.random.fold_in(arg_keys[11], 71), 0)
    key_base = draw_key_base(jax.random.fold_in(arg_keys[11], 71), 0)
    frozen_value_output = normal_values(arg_keys[3], (TOKEN_COUNT, KVH * HD), 1.0, 6.0, ((0, 128),))
    out_grad = normal_values(arg_keys[4], (TOKEN_COUNT, H * HD), 1.0, 6.0, ((0, 128),))
    query_down_factor = normal_values(arg_keys[5], (D, R), D ** -0.5, 0.078125)
    query_up_factor = normal_values(arg_keys[6], (R, H * HD), (4 * R) ** -0.5, 0.375)
    value_down_factor = normal_values(arg_keys[7], (D, R), D ** -0.5, 0.078125)
    value_up_factor = normal_values(arg_keys[8], (R, KVH * HD), (4 * R) ** -0.5, 0.375)
    doc_lengths = ragged_sizes(arg_keys[9], NDOC, TOKEN_COUNT, MOST, 2).astype(jnp.int32)
    stretch_map = draw_stretch_map(jax.random.fold_in(arg_keys[11], 71), 0)
    return dict(normed_input=normed_input, frozen_query_output=frozen_query_output, key_base=key_base, frozen_value_output=frozen_value_output, out_grad=out_grad, query_down_factor=query_down_factor, query_up_factor=query_up_factor, value_down_factor=value_down_factor, value_up_factor=value_up_factor, doc_lengths=doc_lengths, stretch_map=stretch_map)


THETA = 1000000.0
ADAPTER_SCALE = 2.0
NEG_FILL = -1.0e30


def rotate(field, places, turning):
    half_width = field.shape[-1] // 2
    inverse = THETA ** (-jnp.arange(half_width, dtype=jnp.float32) * 2.0 / field.shape[-1])
    angles = places.astype(jnp.float32)[:, None] * inverse[None, :]
    cosine = jnp.cos(angles)[:, None, :]
    sine_part = turning * jnp.sin(angles)[:, None, :]
    first = field[..., :half_width]
    second = field[..., half_width:]
    return jnp.concatenate([first * cosine - second * sine_part, second * cosine + first * sine_part], axis=-1)


def document_of(places, doc_lengths):
    doc_ends = jnp.cumsum(doc_lengths).astype(jnp.int32)
    doc_starts = doc_ends - doc_lengths
    doc_index = jnp.sum((places[:, None] >= doc_ends[None, :]).astype(jnp.int32), axis=1)
    picked = (doc_index[:, None] == jnp.arange(doc_lengths.shape[0], dtype=jnp.int32)[None, :]).astype(jnp.int32)
    offset = jnp.sum(picked * doc_starts[None, :], axis=1)
    return doc_index, places - offset


def group_attention(query_rows, key_block, value_block, grad_rows, allowed, scaling):
    query_wide = query_rows.astype(jnp.float32)
    key_wide = key_block.astype(jnp.float32)
    value_wide = value_block.astype(jnp.float32)
    grad_wide = grad_rows.astype(jnp.float32)
    scores = jnp.einsum('tgd,sd->gts', query_wide, key_wide) * scaling
    scores = jnp.where(allowed[None], scores, NEG_FILL)
    peak_score = jnp.max(scores, axis=-1, keepdims=True)
    weights = jnp.exp(scores - peak_score)
    attention = weights / jnp.sum(weights, axis=-1, keepdims=True)
    attention_low = attention.astype(jnp.bfloat16).astype(jnp.float32)
    attended = jnp.einsum('gts,sd->tgd', attention_low, value_wide).astype(jnp.bfloat16)
    row_dot = jnp.sum(grad_wide * attended.astype(jnp.float32), axis=-1)
    attention_grad = jnp.einsum('tgd,sd->gts', grad_wide, value_wide)
    score_grad = (attention * (attention_grad - jnp.transpose(row_dot)[:, :, None])).astype(jnp.bfloat16).astype(jnp.float32)
    query_gradient = jnp.einsum('gts,sd->tgd', score_grad, key_wide) * scaling
    key_part = jnp.einsum('gts,tgd->sd', score_grad, query_wide) * scaling
    value_part = jnp.einsum('gts,tgd->sd', attention_low, grad_wide)
    return attended, query_gradient, key_part, value_part


def reference(normed_input, frozen_query_output, key_base, frozen_value_output, out_grad, query_down_factor, query_up_factor, value_down_factor, value_up_factor, doc_lengths, stretch_map):
    share = H // KVH
    row_steps = jnp.arange(TOKEN_COUNT, dtype=jnp.int32)
    places = (stretch_map[row_steps // TOK_DEV] * TOK_DEV + row_steps % TOK_DEV).astype(jnp.int32)
    order = jnp.zeros((TOKEN_COUNT,), jnp.int32).at[places].set(row_steps)
    doc_index, local_place = document_of(places, doc_lengths)
    query_adapter_output = jnp.dot(normed_input, query_down_factor, preferred_element_type=jnp.float32).astype(jnp.bfloat16)
    value_adapter_output = jnp.dot(normed_input, value_down_factor, preferred_element_type=jnp.float32).astype(jnp.bfloat16)
    complete_query = frozen_query_output.astype(jnp.float32) + ADAPTER_SCALE * jnp.dot(query_adapter_output, query_up_factor, preferred_element_type=jnp.float32)
    query_rot = rotate(complete_query.reshape(TOKEN_COUNT, H, HD), local_place, 1.0).astype(jnp.bfloat16)
    key_rot = rotate(key_base.astype(jnp.float32).reshape(TOKEN_COUNT, KVH, HD), local_place, 1.0).astype(jnp.bfloat16)
    value_row_matrix = (frozen_value_output.astype(jnp.float32) + ADAPTER_SCALE * jnp.dot(value_adapter_output, value_up_factor, preferred_element_type=jnp.float32)).astype(jnp.bfloat16)
    value_row_matrix = value_row_matrix.reshape(TOKEN_COUNT, KVH, HD)
    query_seq = query_rot[order].reshape(TOKEN_COUNT, KVH, share, HD)
    grad_seq = out_grad[order].reshape(TOKEN_COUNT, KVH, share, HD)
    key_pad = jnp.concatenate([jnp.zeros((MOST, KVH, HD), jnp.bfloat16), key_rot[order]], axis=0)
    value_pad = jnp.concatenate([jnp.zeros((MOST, KVH, HD), jnp.bfloat16), value_row_matrix[order]], axis=0)
    doc_seq = doc_index[order]
    doc_pad = jnp.concatenate([jnp.full((MOST,), -1, jnp.int32), doc_seq.astype(jnp.int32)])
    window = MOST + TOK_DEV
    scaling = HD ** -0.5
    mapped = jax.vmap(group_attention, in_axes=(1, 1, 1, 1, None, None))

    def block_step(carry, index):
        key_acc, value_acc = carry
        start = (index * TOK_DEV).astype(jnp.int32)
        query_block = lax.dynamic_slice_in_dim(query_seq, start, TOK_DEV, 0)
        grad_block = lax.dynamic_slice_in_dim(grad_seq, start, TOK_DEV, 0)
        key_block = lax.dynamic_slice_in_dim(key_pad, start, window, 0)
        value_block = lax.dynamic_slice_in_dim(value_pad, start, window, 0)
        doc_block = lax.dynamic_slice_in_dim(doc_seq, start, TOK_DEV, 0)
        doc_window = lax.dynamic_slice_in_dim(doc_pad, start, window, 0)
        key_places = start - MOST + jnp.arange(window, dtype=jnp.int32)
        query_places = start + jnp.arange(TOK_DEV, dtype=jnp.int32)
        allowed = (doc_window[None, :] == doc_block[:, None]) & (key_places[None, :] <= query_places[:, None]) & (key_places >= 0)[None, :]
        attended, query_gradient, key_part, value_part = mapped(query_block, key_block, value_block, grad_block, allowed, scaling)
        key_old = lax.dynamic_slice_in_dim(key_acc, start, window, 0)
        value_old = lax.dynamic_slice_in_dim(value_acc, start, window, 0)
        key_acc = lax.dynamic_update_slice_in_dim(key_acc, key_old + jnp.transpose(key_part, (1, 0, 2)), start, 0)
        value_acc = lax.dynamic_update_slice_in_dim(value_acc, value_old + jnp.transpose(value_part, (1, 0, 2)), start, 0)
        return (key_acc, value_acc), (jnp.transpose(attended, (1, 0, 2, 3)), jnp.transpose(query_gradient, (1, 0, 2, 3)))

    zeros_acc = jnp.zeros((MOST + TOKEN_COUNT, KVH, HD), jnp.float32)
    (key_acc, value_acc), (attended_blocks, query_blocks) = lax.scan(
        block_step, (zeros_acc, zeros_acc), jnp.arange(TOKEN_COUNT // TOK_DEV, dtype=jnp.int32))
    attended = attended_blocks.reshape(TOKEN_COUNT, H * HD)[places]
    query_grad_seq = query_blocks.reshape(TOKEN_COUNT, H, HD)[places]
    query_gradient = rotate(query_grad_seq, local_place, -1.0).astype(jnp.bfloat16).reshape(TOKEN_COUNT, H * HD)
    key_total = key_acc[MOST:][places]
    value_total = value_acc[MOST:][places]
    key_grad = rotate(key_total, local_place, -1.0).astype(jnp.bfloat16).reshape(TOKEN_COUNT, KVH * HD)
    value_gradient = value_total.reshape(TOKEN_COUNT, KVH * HD).astype(jnp.bfloat16)
    query_lifted = (ADAPTER_SCALE * jnp.dot(query_gradient, query_up_factor.T, preferred_element_type=jnp.float32)).astype(jnp.bfloat16)
    value_lifted = (ADAPTER_SCALE * jnp.dot(value_gradient, value_up_factor.T, preferred_element_type=jnp.float32)).astype(jnp.bfloat16)
    grad_down_q = jnp.dot(normed_input.T, query_lifted, preferred_element_type=jnp.float32) / TOKEN_COUNT
    query_up_gradient = ADAPTER_SCALE * jnp.dot(query_adapter_output.T, query_gradient, preferred_element_type=jnp.float32) / TOKEN_COUNT
    grad_down_v = jnp.dot(normed_input.T, value_lifted, preferred_element_type=jnp.float32) / TOKEN_COUNT
    value_up_gradient = ADAPTER_SCALE * jnp.dot(value_adapter_output.T, value_gradient, preferred_element_type=jnp.float32) / TOKEN_COUNT
    return (attended, key_grad, grad_down_q, query_up_gradient, grad_down_v, value_up_gradient)
```

```python
import functools

import jax
import jax.numpy as jnp
from jax import lax
from jax.experimental import pallas as pl
from jax.experimental.pallas import tpu as pltpu
from jax.sharding import PartitionSpec as P

HD = 128
RANK = 64
TOK = 256
SUB = 128
REACH = 1152
SPANK = 5 * TOK
ROWS = 7 * TOK
KP = 384
HEADS = 8
SHARE = 5
COUNTS = (2, 3, 3)
THETA = 1000000.0
ADAPTER_SCALE = 2.0
LOG2E = 1.4426950408889634
NEG = -1e30
BF = jnp.bfloat16
F32 = jnp.float32


def mm(a, b):
    return lax.dot_general(a, b, (((1,), (0,)), ((), ())), preferred_element_type=F32)


def mm_nt(a, b):
    return lax.dot_general(a, b, (((1,), (1,)), ((), ())), preferred_element_type=F32)


def mm_tn(a, b):
    return lax.dot_general(a, b, (((0,), (0,)), ((), ())), preferred_element_type=F32)


def attention_kernel(share, first_call, sc, fq, og, lora, qup, vup, cos, sin, dst, *rest):
    kin, vin, lin = rest[0:6], rest[6:12], rest[12:18]
    rest = rest[18:] if first_call else rest[19:]
    att, dkm, dko, liftq, qupg, vupg, lvm, lvo = rest[0:8]
    kx, vx, kt, vt, lt, bias, ss, dp, dka, dva, qn, dn, dnt, dqn, lva = rest[8:]
    g = pl.program_id(0)
    groups = pl.num_programs(0)
    wide = share * SUB
    scale = HD ** (-0.5)
    cexp = scale * LOG2E
    shift = pl.multiple_of(sc[0], TOK)

    def place(target, refs):
        for chip in range(3):
            low = pl.multiple_of((2 - chip) * 2 * TOK + shift, TOK)
            mine, other = refs[2 * chip], refs[2 * chip + 1]

            @pl.when(sc[1 + chip] == 0)
            def _():
                target[pl.ds(low, TOK), :] = mine[...]
                target[pl.ds(low + TOK, TOK), :] = other[...]

            @pl.when(sc[1 + chip] != 0)
            def _():
                target[pl.ds(low, TOK), :] = other[...]
                target[pl.ds(low + TOK, TOK), :] = mine[...]

    def take(read, mine, other):
        for chip in range(3):
            low = pl.multiple_of((2 - chip) * 2 * TOK + shift, TOK)

            @pl.when(sc[1 + chip] == 0)
            def _():
                mine[chip] = read(pl.ds(low, TOK))
                other[chip] = read(pl.ds(low + TOK, TOK))

            @pl.when(sc[1 + chip] != 0)
            def _():
                mine[chip] = read(pl.ds(low + TOK, TOK))
                other[chip] = read(pl.ds(low, TOK))

    @pl.when(g == 0)
    def _():
        for piece in (slice(0, TOK), slice(TOK + SPANK, ROWS)):
            dka[piece, :] = jnp.zeros((TOK, HD), F32)
            dva[piece, :] = jnp.zeros((TOK, HD), F32)
        lva[...] = jnp.zeros_like(lva)
        liftq[...] = jnp.zeros_like(liftq)
        place(kx, lin)
        lt[...] = kx[TOK : TOK + SPANK, :].T
        for b in range(2):
            first = dst[0:1, b * SUB : (b + 1) * SUB]
            last = SPANK - 2 * SUB + b * SUB + lax.broadcasted_iota(jnp.int32, (1, SUB), 1)
            key_at = b * SUB + lax.broadcasted_iota(jnp.int32, (REACH, SUB), 0)
            bias[b] = jnp.where((key_at >= first) & (key_at <= last), 0.0, NEG)

    place(kx, kin)
    place(vx, vin)
    kt[...] = kx[TOK : TOK + SPANK, :].T
    vt[...] = vx[TOK : TOK + SPANK, :].T
    lora_q = lora[:, 0:RANK]
    extra = mm(lora_q, qup[...])
    for h in range(share):
        col = slice(h * HD, (h + 1) * HD)
        u = fq[:, col].astype(F32) + ADAPTER_SCALE * extra[:, col]
        qr = (u * cos[...] + pltpu.roll(u, HD // 2, 1) * sin[...]).astype(BF)
        for b in range(2):
            qn[b, h * SUB : (h + 1) * SUB, :] = qr[b * SUB : (b + 1) * SUB]
            dn[b, h * SUB : (h + 1) * SUB, :] = og[b * SUB : (b + 1) * SUB, col]
    pieces = [slice(i, i + KP) for i in range(0, REACH, KP)]

    keep = {}

    def phase_a(b):
        dnt[b] = dn[b].astype(F32).T
        at = TOK + b * SUB
        top = None
        for piece in pieces:
            s = mm_nt(kx[at + piece.start : at + piece.stop, :], qn[b])
            s = s + jnp.concatenate([bias[b, piece, :]] * share, axis=1)
            ss[b, piece, :] = s
            t = jnp.max(s.reshape(KP // 8, 8, wide), axis=0)
            top = t if top is None else jnp.maximum(top, t)
        keep["top", b] = jnp.max(top, axis=0, keepdims=True) * cexp

    def phase_p(b):
        at = TOK + b * SUB
        for piece in pieces:
            dp[b, piece, :] = mm_nt(vx[at + piece.start : at + piece.stop, :], dn[b])

    def phase_b(b):
        total = None
        for piece in pieces:
            e = jnp.exp2(ss[b, piece, :] * cexp - keep["top", b])
            ss[b, piece, :] = e
            t = jnp.sum(e.reshape(KP // 8, 8, wide), axis=0)
            total = t if total is None else total + t
        keep["inverse", b] = 1.0 / jnp.sum(total, axis=0, keepdims=True)

    def add(target, b, piece, value):
        rows = slice(TOK + b * SUB + piece.start, TOK + b * SUB + piece.stop)
        if b == 0:
            target[rows, :] = value
        elif piece.stop < REACH:
            target[rows, :] += value
        else:
            cut = KP - SUB
            target[rows.start : rows.start + cut, :] += value[:cut]
            target[rows.start + cut : rows.stop, :] = value[cut:]

    def phase_c(b):
        ot = None
        for piece in pieces:
            pb = (ss[b, piece, :] * keep["inverse", b]).astype(BF)
            t = mm(vt[:, b * SUB + piece.start : b * SUB + piece.stop], pb)
            ot = t if ot is None else ot + t
            add(dva, b, piece, mm(pb, dn[b]))
        ob = ot.astype(BF).astype(F32)
        keep["dot", b] = jnp.sum(dnt[b] * ob, axis=0, keepdims=True)
        obn = ob.T.astype(BF)
        for h in range(share):
            att[b * SUB : (b + 1) * SUB, h * HD : (h + 1) * HD] = obn[h * SUB : (h + 1) * SUB]

    def phase_d(b):
        qt = None
        for piece in pieces:
            ds = ((ss[b, piece, :] * keep["inverse", b]) * (dp[b, piece, :] - keep["dot", b])).astype(BF)
            t = mm(kt[:, b * SUB + piece.start : b * SUB + piece.stop], ds)
            qt = t if qt is None else qt + t
            add(dka, b, piece, mm(ds, qn[b]))
        dq = qt.T * scale
        rows = slice(b * SUB, (b + 1) * SUB)
        for h in range(share):
            u = dq[h * SUB : (h + 1) * SUB]
            dqn[rows, h * HD : (h + 1) * HD] = (
                u * cos[rows, :] - pltpu.roll(u, HD // 2, 1) * sin[rows, :]
            ).astype(BF)

    phase_a(0)
    phase_b(0)
    phase_a(1)
    phase_p(0)
    phase_c(0)
    phase_b(1)
    phase_p(1)
    phase_d(0)
    phase_c(1)
    phase_d(1)

    dqb = dqn[...]
    liftq[...] += mm_nt(dqb, qup[...])
    lora_t = lora[...].astype(F32).T[0:RANK].astype(BF)
    up = mm(lora_t, dqb)
    for h in range(share):
        qupg[h] = (ADAPTER_SCALE * up[:, h * HD : (h + 1) * HD]).astype(qupg.dtype)
    dvb = dva[TOK : TOK + SPANK, :].astype(BF)
    lva[TOK : TOK + SPANK, :] += mm_nt(dvb, vup[...])
    vupg[0] = (ADAPTER_SCALE * mm(lt[...], dvb)[RANK : 2 * RANK]).astype(vupg.dtype)
    take(lambda rows: (dka[rows, :] * scale).astype(BF), dkm, dko)

    @pl.when(g == groups - 1)
    def _():
        take(lambda rows: lva[rows, :], lvm, lvo)


def prepare_kernel(normed, qdown, vdown, keys, values, vup, cos, sin, *outs):
    lora_q = mm(normed[...], qdown[...]).astype(BF)
    lora_v = mm(normed[...], vdown[...]).astype(BF)
    head = 0
    for place, count in enumerate(COUNTS):
        out = outs[place]
        for c in range(count):
            col = slice((head + c) * HD, (head + c + 1) * HD)
            k = keys[:, col].astype(F32)
            k = k * cos[...] + pltpu.roll(k, HD // 2, 1) * sin[...]
            out[:, c * HD : (c + 1) * HD] = k.astype(BF)
            v = values[:, col].astype(F32) + ADAPTER_SCALE * mm(lora_v, vup[:, col])
            out[:, (count + c) * HD : (count + c + 1) * HD] = v.astype(BF)
        if place == 0:
            out[:, 2 * count * HD : 2 * count * HD + RANK] = lora_q
            out[:, 2 * count * HD + RANK : 2 * count * HD + 2 * RANK] = lora_v
        head += count


def prepare(*operands):
    vmem = pl.BlockSpec(memory_space=pltpu.VMEM)
    widths = [2 * count * HD + (HD if place == 0 else 0) for place, count in enumerate(COUNTS)]
    return pl.pallas_call(
        prepare_kernel,
        out_shape=[jax.ShapeDtypeStruct((TOK, width), BF) for width in widths],
        in_specs=[vmem] * len(operands),
        out_specs=[vmem] * len(widths),
        compiler_params=pltpu.CompilerParams(vmem_limit_bytes=40 * 2**20),
        name="prepare",
    )(*operands)


def attention(scalars, frozen, grad, own, qup, vup, cos, sin, dst, keyed, lorad, attended, first, count):
    share = SHARE
    wide = share * HD
    tail = 2 * COUNTS[0]

    def whole(shape):
        return pl.BlockSpec(shape, lambda g, s: (0,) * len(shape))

    def column(rows, width, offset):
        return pl.BlockSpec((rows, width), lambda g, s: (0, g + offset))

    lora_spec = pl.BlockSpec((TOK, HD), lambda g, s: (0, tail))
    in_specs = [
        column(TOK, wide, first), column(TOK, wide, first), lora_spec,
        column(RANK, wide, first), column(RANK, HD, first),
        whole((TOK, HD)), whole((TOK, HD)), whole((1, TOK)),
    ]
    in_specs += [column(TOK, HD, 0)] * 6 + [column(TOK, HD, count)] * 6 + [lora_spec] * 6
    operands = [scalars, frozen, grad, own, qup, vup, cos, sin, dst, *keyed, *keyed, *lorad]
    aliases = {}
    if attended is not None:
        aliases = {len(operands): 0}
        operands.append(attended)
        in_specs.append(pl.BlockSpec(memory_space=pl.ANY))
    pair = jax.ShapeDtypeStruct((3, TOK, count * HD), BF)
    lift = jax.ShapeDtypeStruct((3, TOK, RANK), F32)
    out_shape = [
        jax.ShapeDtypeStruct(frozen.shape, BF), pair, pair,
        jax.ShapeDtypeStruct((TOK, RANK), F32),
        jax.ShapeDtypeStruct((count * share, RANK, HD), BF),
        jax.ShapeDtypeStruct((count, RANK, HD), BF), lift, lift,
    ]
    pair_spec = pl.BlockSpec((3, TOK, HD), lambda g, s: (0, 0, g))
    out_specs = [
        column(TOK, wide, first), pair_spec, pair_spec, whole((TOK, RANK)),
        pl.BlockSpec((share, RANK, HD), lambda g, s: (g, 0, 0)),
        pl.BlockSpec((1, RANK, HD), lambda g, s: (g, 0, 0)),
        whole((3, TOK, RANK)), whole((3, TOK, RANK)),
    ]
    wide_rows = share * SUB
    scratch = [
        pltpu.VMEM((ROWS, HD), BF), pltpu.VMEM((ROWS, HD), BF),
        pltpu.VMEM((HD, SPANK), BF), pltpu.VMEM((HD, SPANK), BF), pltpu.VMEM((HD, SPANK), BF),
        pltpu.VMEM((2, REACH, SUB), F32),
        pltpu.VMEM((2, REACH, wide_rows), F32), pltpu.VMEM((2, REACH, wide_rows), F32),
        pltpu.VMEM((ROWS, HD), F32), pltpu.VMEM((ROWS, HD), F32),
        pltpu.VMEM((2, wide_rows, HD), BF), pltpu.VMEM((2, wide_rows, HD), BF),
        pltpu.VMEM((2, HD, wide_rows), F32), pltpu.VMEM((TOK, wide), BF),
        pltpu.VMEM((ROWS, RANK), F32),
    ]
    return pl.pallas_call(
        functools.partial(attention_kernel, share, attended is None),
        out_shape=out_shape,
        grid_spec=pltpu.PrefetchScalarGridSpec(
            num_scalar_prefetch=1, grid=(count,), in_specs=in_specs, out_specs=out_specs, scratch_shapes=scratch
        ),
        input_output_aliases=aliases,
        compiler_params=pltpu.CompilerParams(
            dimension_semantics=("arbitrary",), vmem_limit_bytes=40 * 2**20
        ),
        cost_estimate=pl.CostEstimate(
            flops=12 * 2 * REACH * SUB * share * HD * count, transcendentals=2 * REACH * SUB * share * count,
            bytes_accessed=6 * 2**20 * count // HEADS,
        ),
        name="attention",
    )(*operands)


def moved(block, step):
    devices = range(lax.axis_size("ctx"))
    route = [(i, step(i)) for i in devices if step(i) in devices]
    return lax.ppermute(block, "ctx", route)


def twin(block):
    return moved(block, lambda i: i ^ 1)


def ahead(block, chips):
    return moved(block, lambda i: i + 2 * chips)


def on_device(
    normed_input,
    frozen_query_output,
    key_base,
    frozen_value_output,
    out_grad,
    query_down_factor,
    query_up_factor,
    value_down_factor,
    value_up_factor,
    doc_lengths,
    stretch_map,
):
    devices = lax.axis_size("ctx")
    mine = lax.axis_index("ctx")
    chip, core = mine // 2, mine % 2
    stretch = stretch_map[mine]
    steps = jnp.arange(TOK, dtype=jnp.int32)
    places = stretch * TOK + steps
    documents = jnp.arange(doc_lengths.shape[0], dtype=jnp.int32)
    ends = jnp.sum(jnp.where(documents[:, None] >= documents[None, :], doc_lengths[None, :], 0), axis=1)
    starts = jnp.max(jnp.where(ends[None, :] <= places[:, None], ends[None, :], 0), axis=1)
    local = places - starts
    reach = 4 * TOK + steps - local
    half = HD // 2
    inverse = THETA ** (-jnp.arange(half, dtype=F32) * 2.0 / HD)
    angles = local.astype(F32)[:, None] * inverse[None, :]
    cosine, sine = jnp.cos(angles), jnp.sin(angles)
    cos = jnp.concatenate([cosine, cosine], axis=1)
    sin = jnp.concatenate([-sine, sine], axis=1)
    chips = chip - jnp.arange(3, dtype=jnp.int32)
    flips = (core + stretch_map[2 * jnp.maximum(chips, 0)]) % 2
    scalars = jnp.concatenate([(TOK * (1 - stretch % 2))[None], flips]).astype(jnp.int32)

    payloads = prepare(
        normed_input, query_down_factor, value_down_factor, key_base, frozen_value_output, value_up_factor, cos, sin
    )
    windows = []
    for payload in payloads:
        near, far = ahead(payload, 1), ahead(payload, 2)
        windows.append([payload, twin(payload), near, twin(near), far, twin(far)])
    attended = None
    first = 0
    key_parts, lift_q, lift_mine, lift_other, query_ups, value_ups = [], 0.0, 0.0, 0.0, [], []
    for place, count in enumerate(COUNTS):
        attended, key_mine, key_other, lq, qu, vu, lm, lo = attention(
            scalars, frozen_query_output, out_grad, payloads[0], query_up_factor, value_up_factor,
            cos, sin, reach[None, :], windows[place], windows[0], attended, first, count,
        )
        first += count
        lift_q, lift_mine, lift_other = lift_q + lq, lift_mine + lm, lift_other + lo
        query_ups.append(qu)
        value_ups.append(vu)
        if place == len(COUNTS) - 1:
            key_mine = jnp.concatenate([key_mine, lift_mine.astype(BF)], axis=2)
            key_other = jnp.concatenate([key_other, lift_other.astype(BF)], axis=2)
        both = key_mine.astype(F32) + twin(key_other).astype(F32)
        near = ahead(both[1].astype(BF), -1)
        far = ahead(both[2].astype(BF), -2)
        key_parts.append(both[0] + near.astype(F32) + far.astype(F32))
    total = jnp.concatenate(key_parts, axis=1)
    key_total = total[:, : HEADS * HD].reshape(TOK, HEADS, HD)
    swapped = jnp.concatenate([key_total[..., half:], key_total[..., :half]], axis=-1)
    key_grad = (key_total * cos[:, None, :] - swapped * sin[:, None, :]).astype(BF).reshape(TOK, HEADS * HD)
    lift_q = (ADAPTER_SCALE * lift_q).astype(BF)
    lift_v = (ADAPTER_SCALE * total[:, HEADS * HD :]).astype(BF)
    lifts = jnp.concatenate([lift_q, lift_v], axis=1)
    width = normed_input.shape[1]
    tiles = width // HD
    downs = jnp.einsum("tr,td->rd", lifts, normed_input, preferred_element_type=F32).astype(BF)
    downs = jnp.transpose(downs.reshape(2 * RANK, tiles, HD), (1, 0, 2)).reshape(-1, HD)
    terms = jnp.concatenate([downs] + [x.reshape(-1, HD) for x in query_ups + value_ups], axis=0)
    rows = terms.shape[0] // devices
    spread = lax.all_to_all(terms.reshape(devices, rows, HD), "ctx", 0, 0)
    summed = jnp.sum(spread.astype(F32), axis=0).astype(BF)
    whole = lax.all_to_all(jnp.broadcast_to(summed[None], (devices, rows, HD)), "ctx", 0, 0).reshape(-1, HD)
    whole = whole.astype(F32) / (TOK * devices)
    downs = jnp.transpose(whole[: tiles * 2 * RANK].reshape(tiles, 2 * RANK, HD), (0, 2, 1)).reshape(width, 2 * RANK)
    ups = jnp.transpose(whole[tiles * 2 * RANK :].reshape(-1, RANK, HD), (1, 0, 2)).reshape(RANK, -1)
    query_width = HEADS * SHARE * HD
    return (attended, key_grad, downs[:, :RANK], ups[:, :query_width], downs[:, RANK:], ups[:, query_width:])


def solution(mesh):
    row = P("ctx", None)
    return jax.shard_map(
        on_device,
        mesh=mesh,
        in_specs=(row, row, row, row, row, P(), P(), P(), P(), P(), P()),
        out_specs=(row, row, P(), P(), P(), P()),
        check_vma=False,
    )
```

```python
import functools

import jax
import jax.numpy as jnp
from jax import lax
from jax.experimental import pallas as pl
from jax.experimental.pallas import tpu as pltpu
from jax.sharding import PartitionSpec as P

HD = 128
RANK = 64
TOK = 256
SUB = 128
REACH = 1152
SPANK = 5 * TOK
ROWS = 7 * TOK
KP = 384
HEADS = 8
SHARE = 5
COUNTS = (3, 5)
UNIT = SHARE + 1
EDGE = UNIT * HEADS
VMEM_ASK = 60 * 2**20
THETA = 1000000.0
ADAPTER_SCALE = 2.0
LOG2E = 1.4426950408889634
NEG = -1e30
BF = jnp.bfloat16
F32 = jnp.float32


def mm(a, b):
    return lax.dot_general(a, b, (((1,), (0,)), ((), ())), preferred_element_type=F32)


def mm_nt(a, b):
    return lax.dot_general(a, b, (((1,), (1,)), ((), ())), preferred_element_type=F32)


def mm_tn(a, b):
    return lax.dot_general(a, b, (((0,), (0,)), ((), ())), preferred_element_type=F32)


def attention_kernel(share, first_call, sc, query, og, lora, qup, vup, cos, sin, dst, *rest):
    kin, vin, lin = rest[0:6], rest[6:12], rest[12:18]
    rest = rest[18:] if first_call else rest[22:]
    att, dkm, dko, terms, liftq, lvm, lvo = rest[0:7]
    kx, vx, kt, vt, lt, bias, ss, dp, dka, dva, qn, dn, dnt, dqn, lva = rest[7:]
    g = pl.program_id(0)
    groups = pl.num_programs(0)
    wide = share * SUB
    scale = HD ** (-0.5)
    cexp = scale * LOG2E
    shift = pl.multiple_of(sc[0], TOK)

    def place(target, refs):
        for chip in range(3):
            low = pl.multiple_of((2 - chip) * 2 * TOK + shift, TOK)
            mine, other = refs[2 * chip], refs[2 * chip + 1]

            @pl.when(sc[1 + chip] == 0)
            def _():
                target[pl.ds(low, TOK), :] = mine[...]
                target[pl.ds(low + TOK, TOK), :] = other[...]

            @pl.when(sc[1 + chip] != 0)
            def _():
                target[pl.ds(low, TOK), :] = other[...]
                target[pl.ds(low + TOK, TOK), :] = mine[...]

    def take(read, mine, other):
        for chip in range(3):
            low = pl.multiple_of((2 - chip) * 2 * TOK + shift, TOK)

            @pl.when(sc[1 + chip] == 0)
            def _():
                mine[chip] = read(pl.ds(low, TOK))
                other[chip] = read(pl.ds(low + TOK, TOK))

            @pl.when(sc[1 + chip] != 0)
            def _():
                mine[chip] = read(pl.ds(low + TOK, TOK))
                other[chip] = read(pl.ds(low, TOK))

    @pl.when(g == 0)
    def _():
        for piece in (slice(0, TOK), slice(TOK + SPANK, ROWS)):
            dka[piece, :] = jnp.zeros((TOK, HD), F32)
            dva[piece, :] = jnp.zeros((TOK, HD), F32)
        lva[...] = jnp.zeros_like(lva)
        liftq[...] = jnp.zeros_like(liftq)
        place(kx, lin)
        lt[...] = kx[TOK : TOK + SPANK, :].T
        for b in range(2):
            first = dst[0:1, b * SUB : (b + 1) * SUB]
            last = SPANK - 2 * SUB + b * SUB + lax.broadcasted_iota(jnp.int32, (1, SUB), 1)
            key_at = b * SUB + lax.broadcasted_iota(jnp.int32, (REACH, SUB), 0)
            bias[b] = jnp.where((key_at >= first) & (key_at <= last), 0.0, NEG)

    place(kx, kin)
    place(vx, vin)
    kt[...] = kx[TOK : TOK + SPANK, :].T
    vt[...] = vx[TOK : TOK + SPANK, :].T
    for h in range(share):
        col = slice(h * HD, (h + 1) * HD)
        for b in range(2):
            qn[b, h * SUB : (h + 1) * SUB, :] = query[b * SUB : (b + 1) * SUB, col]
            dn[b, h * SUB : (h + 1) * SUB, :] = og[b * SUB : (b + 1) * SUB, col]
    pieces = [slice(i, i + KP) for i in range(0, REACH, KP)]

    keep = {}

    def phase_a(b):
        dnt[b] = dn[b].astype(F32).T
        at = TOK + b * SUB
        top = None
        for piece in pieces:
            s = mm_nt(kx[at + piece.start : at + piece.stop, :], qn[b])
            s = s + jnp.concatenate([bias[b, piece, :]] * share, axis=1)
            ss[b, piece, :] = s
            t = jnp.max(s.reshape(KP // 8, 8, wide), axis=0)
            top = t if top is None else jnp.maximum(top, t)
        keep["top", b] = jnp.max(top, axis=0, keepdims=True) * cexp

    def phase_p(b):
        at = TOK + b * SUB
        for piece in pieces:
            dp[b, piece, :] = mm_nt(vx[at + piece.start : at + piece.stop, :], dn[b])

    def phase_b(b):
        total = None
        for piece in pieces:
            e = jnp.exp2(ss[b, piece, :] * cexp - keep["top", b])
            ss[b, piece, :] = e
            t = jnp.sum(e.reshape(KP // 8, 8, wide), axis=0)
            total = t if total is None else total + t
        keep["inverse", b] = 1.0 / jnp.sum(total, axis=0, keepdims=True)

    def add(target, b, piece, value):
        rows = slice(TOK + b * SUB + piece.start, TOK + b * SUB + piece.stop)
        if b == 0:
            target[rows, :] = value
        elif piece.stop < REACH:
            target[rows, :] += value
        else:
            cut = KP - SUB
            target[rows.start : rows.start + cut, :] += value[:cut]
            target[rows.start + cut : rows.stop, :] = value[cut:]

    def phase_c(b):
        ot = None
        for piece in pieces:
            pb = (ss[b, piece, :] * keep["inverse", b]).astype(BF)
            t = mm(vt[:, b * SUB + piece.start : b * SUB + piece.stop], pb)
            ot = t if ot is None else ot + t
            add(dva, b, piece, mm(pb, dn[b]))
        ob = ot.astype(BF).astype(F32)
        keep["dot", b] = jnp.sum(dnt[b] * ob, axis=0, keepdims=True)
        obn = ob.T.astype(BF)
        for h in range(share):
            att[b * SUB : (b + 1) * SUB, h * HD : (h + 1) * HD] = obn[h * SUB : (h + 1) * SUB]

    def phase_d(b):
        qt = None
        for piece in pieces:
            ds = ((ss[b, piece, :] * keep["inverse", b]) * (dp[b, piece, :] - keep["dot", b])).astype(BF)
            t = mm(kt[:, b * SUB + piece.start : b * SUB + piece.stop], ds)
            qt = t if qt is None else qt + t
            add(dka, b, piece, mm(ds, qn[b]))
        dq = qt.T * scale
        rows = slice(b * SUB, (b + 1) * SUB)
        for h in range(share):
            u = dq[h * SUB : (h + 1) * SUB]
            dqn[rows, h * HD : (h + 1) * HD] = (
                u * cos[rows, :] - pltpu.roll(u, HD // 2, 1) * sin[rows, :]
            ).astype(BF)

    phase_a(0)
    phase_b(0)
    phase_a(1)
    phase_p(0)
    phase_c(0)
    phase_b(1)
    phase_p(1)
    phase_d(0)
    phase_c(1)
    phase_d(1)

    dqb = dqn[...]
    liftq[...] += mm_nt(dqb, qup[...])
    lora_t = lora[...].astype(F32).T[0:RANK].astype(BF)
    up = mm(lora_t, dqb)
    for h in range(share):
        terms[h] = (ADAPTER_SCALE * up[:, h * HD : (h + 1) * HD]).astype(BF)
    dvb = dva[TOK : TOK + SPANK, :].astype(BF)
    lva[TOK : TOK + SPANK, :] += mm_nt(dvb, vup[...])
    terms[share] = (ADAPTER_SCALE * mm(lt[...], dvb)[RANK : 2 * RANK]).astype(BF)
    take(lambda rows: (dka[rows, :] * scale).astype(BF), dkm, dko)

    @pl.when(g == groups - 1)
    def _():
        take(lambda rows: lva[rows, :], lvm, lvo)


def prepare_kernel(normed, qdown, vdown, keys, values, vup, cos, sin, *outs):
    lora = mm_nt(normed[...], jnp.concatenate([qdown[...], vdown[...]], axis=0)).astype(BF)
    lora_v = lora[:, RANK:]
    head = 0
    for place, count in enumerate(COUNTS):
        out = outs[place]
        for c in range(count):
            col = slice((head + c) * HD, (head + c + 1) * HD)
            k = keys[:, col].astype(F32)
            k = k * cos[...] + pltpu.roll(k, HD // 2, 1) * sin[...]
            out[:, c * HD : (c + 1) * HD] = k.astype(BF)
            v = values[:, col].astype(F32) + ADAPTER_SCALE * mm(lora_v, vup[:, col])
            out[:, (count + c) * HD : (count + c + 1) * HD] = v.astype(BF)
        if place == 0:
            out[:, 2 * count * HD : (2 * count + 1) * HD] = lora
        head += count


def prepare(*operands):
    vmem = pl.BlockSpec(memory_space=pltpu.VMEM)
    widths = [2 * count * HD + (HD if place == 0 else 0) for place, count in enumerate(COUNTS)]
    return pl.pallas_call(
        prepare_kernel,
        out_shape=[jax.ShapeDtypeStruct((TOK, width), BF) for width in widths],
        in_specs=[vmem] * len(operands),
        out_specs=[vmem] * len(widths),
        compiler_params=pltpu.CompilerParams(vmem_limit_bytes=VMEM_ASK),
        name="prepare",
    )(*operands)


def rotate_kernel(frozen, lora, qup, cos, sin, query):
    extra = mm(lora[:, 0:RANK], qup[...])
    for h in range(SHARE):
        col = slice(h * HD, (h + 1) * HD)
        u = frozen[:, col].astype(F32) + ADAPTER_SCALE * extra[:, col]
        query[:, col] = (u * cos[...] + pltpu.roll(u, HD // 2, 1) * sin[...]).astype(BF)


def rotate_queries(frozen, own, qup, cos, sin):
    wide = SHARE * HD
    tail = 2 * COUNTS[0]
    table = pl.BlockSpec((TOK, HD), lambda g: (0, 0))
    return pl.pallas_call(
        rotate_kernel,
        out_shape=jax.ShapeDtypeStruct(frozen.shape, BF),
        grid=(HEADS,),
        in_specs=[
            pl.BlockSpec((TOK, wide), lambda g: (0, g)), pl.BlockSpec((TOK, HD), lambda g: (0, tail)),
            pl.BlockSpec((RANK, wide), lambda g: (0, g)), table, table,
        ],
        out_specs=pl.BlockSpec((TOK, wide), lambda g: (0, g)),
        compiler_params=pltpu.CompilerParams(vmem_limit_bytes=VMEM_ASK),
        name="rotate_queries",
    )(frozen, own, qup, cos, sin)


def gradients_kernel(core, lift_q, lift_v, normed, heads, kept, given):
    down = mm_tn(jnp.concatenate([lift_q[...], lift_v[...]], axis=1), normed[...]).astype(BF)
    tiles = down.shape[1] // HD

    def write(low, high):
        for place, out in enumerate((low, high)):
            out[0 : EDGE // 2] = heads[place * EDGE // 2 : (place + 1) * EDGE // 2]
            for i in range(tiles // 2):
                col = slice((place * tiles // 2 + i) * HD, (place * tiles // 2 + i + 1) * HD)
                out[EDGE // 2 + i] = down[:RANK, col]
                out[EDGE // 2 + tiles // 2 + i] = down[RANK:, col]

    @pl.when(core[0] == 0)
    def _():
        write(kept, given)

    @pl.when(core[0] != 0)
    def _():
        write(given, kept)


def gradients(core, lift_q, lift_v, normed, heads):
    vmem = pl.BlockSpec(memory_space=pltpu.VMEM)
    half = jax.ShapeDtypeStruct((EDGE // 2 + normed.shape[1] // HD, RANK, HD), BF)
    return pl.pallas_call(
        gradients_kernel,
        out_shape=[half, half],
        in_specs=[pl.BlockSpec(memory_space=pltpu.SMEM)] + [vmem] * 4,
        out_specs=[vmem] * 2,
        compiler_params=pltpu.CompilerParams(vmem_limit_bytes=24 * 2**20),
        name="gradients",
    )(core, lift_q, lift_v, normed, heads)


def sum_kernel(spread, out):
    total = jnp.zeros(out.shape[1:], F32)
    for i in range(spread.shape[0]):
        total = total + spread[i].astype(F32)
    low = total.astype(BF)
    for i in range(spread.shape[0]):
        out[i] = low


def sum_and_copy(spread):
    vmem = pl.BlockSpec(memory_space=pltpu.VMEM)
    return pl.pallas_call(
        sum_kernel, out_shape=jax.ShapeDtypeStruct(spread.shape, BF), in_specs=[vmem], out_specs=vmem, name="sum_and_copy"
    )(spread)


def finish_kernel(scale, core, mine, other, down_q, up_q, down_v, up_v):
    def write(low, high):
        for place, half in enumerate((low, high)):
            for i in range(HEADS // 2):
                h = place * HEADS // 2 + i
                for c in range(SHARE):
                    at = (h * SHARE + c) * HD
                    up_q[:, at : at + HD] = half[i * UNIT + c].astype(F32) * scale
                up_v[:, h * HD : (h + 1) * HD] = half[i * UNIT + SHARE].astype(F32) * scale
            tiles = down_q.shape[1] // HD // 2
            for i in range(tiles):
                col = slice((place * tiles + i) * HD, (place * tiles + i + 1) * HD)
                down_q[:, col] = half[EDGE // 2 + i].astype(F32) * scale
                down_v[:, col] = half[EDGE // 2 + tiles + i].astype(F32) * scale

    @pl.when(core[0] == 0)
    def _():
        write(mine, other)

    @pl.when(core[0] != 0)
    def _():
        write(other, mine)


def finish(core, mine, other, tokens, width):
    vmem = pl.BlockSpec(memory_space=pltpu.VMEM)
    query = jax.ShapeDtypeStruct((RANK, HEADS * SHARE * HD), F32)
    down = jax.ShapeDtypeStruct((RANK, width), F32)
    value = jax.ShapeDtypeStruct((RANK, HEADS * HD), F32)
    return pl.pallas_call(
        functools.partial(finish_kernel, 1.0 / tokens),
        out_shape=[down, query, down, value],
        in_specs=[pl.BlockSpec(memory_space=pltpu.SMEM), vmem, vmem],
        out_specs=[vmem] * 4,
        compiler_params=pltpu.CompilerParams(vmem_limit_bytes=VMEM_ASK),
        name="finish",
    )(core, mine, other)


def attention(scalars, query, grad, own, qup, vup, cos, sin, dst, keyed, lorad, held, first, count):
    share = SHARE
    wide = share * HD
    tail = 2 * COUNTS[0]

    def whole(shape):
        return pl.BlockSpec(shape, lambda g, s: (0,) * len(shape))

    def column(rows, width, offset):
        return pl.BlockSpec((rows, width), lambda g, s: (0, g + offset))

    lora_spec = pl.BlockSpec((TOK, HD), lambda g, s: (0, tail))
    in_specs = [
        column(TOK, wide, first), column(TOK, wide, first), lora_spec,
        column(RANK, wide, first), column(RANK, HD, first),
        whole((TOK, HD)), whole((TOK, HD)), whole((1, TOK)),
    ]
    in_specs += [column(TOK, HD, 0)] * 6 + [column(TOK, HD, count)] * 6 + [lora_spec] * 6
    operands = [scalars, query, grad, own, qup, vup, cos, sin, dst, *keyed, *keyed, *lorad]
    aliases = {}
    if held is not None:
        aliases = {len(operands) + i: i for i in range(len(held))}
        operands += held
        in_specs += [pl.BlockSpec(memory_space=pl.ANY)] * len(held)
    pair = jax.ShapeDtypeStruct((3, TOK, HEADS * HD), BF)
    lift = jax.ShapeDtypeStruct((3, TOK, RANK), F32)
    out_shape = [
        jax.ShapeDtypeStruct(query.shape, BF), pair, pair, jax.ShapeDtypeStruct((EDGE, RANK, HD), BF),
        jax.ShapeDtypeStruct((TOK, RANK), F32), lift, lift,
    ]
    pair_spec = pl.BlockSpec((3, TOK, HD), lambda g, s: (0, 0, g + first))
    out_specs = [
        column(TOK, wide, first), pair_spec, pair_spec,
        pl.BlockSpec((UNIT, RANK, HD), lambda g, s: (g + first, 0, 0)),
        whole((TOK, RANK)), whole((3, TOK, RANK)), whole((3, TOK, RANK)),
    ]
    wide_rows = share * SUB
    scratch = [
        pltpu.VMEM((ROWS, HD), BF), pltpu.VMEM((ROWS, HD), BF),
        pltpu.VMEM((HD, SPANK), BF), pltpu.VMEM((HD, SPANK), BF), pltpu.VMEM((HD, SPANK), BF),
        pltpu.VMEM((2, REACH, SUB), F32),
        pltpu.VMEM((2, REACH, wide_rows), F32), pltpu.VMEM((2, REACH, wide_rows), F32),
        pltpu.VMEM((ROWS, HD), F32), pltpu.VMEM((ROWS, HD), F32),
        pltpu.VMEM((2, wide_rows, HD), BF), pltpu.VMEM((2, wide_rows, HD), BF),
        pltpu.VMEM((2, HD, wide_rows), F32), pltpu.VMEM((TOK, wide), BF),
        pltpu.VMEM((ROWS, RANK), F32),
    ]
    return pl.pallas_call(
        functools.partial(attention_kernel, share, held is None),
        out_shape=out_shape,
        grid_spec=pltpu.PrefetchScalarGridSpec(
            num_scalar_prefetch=1, grid=(count,), in_specs=in_specs, out_specs=out_specs, scratch_shapes=scratch
        ),
        input_output_aliases=aliases,
        compiler_params=pltpu.CompilerParams(
            dimension_semantics=("arbitrary",), vmem_limit_bytes=VMEM_ASK
        ),
        cost_estimate=pl.CostEstimate(
            flops=12 * 2 * REACH * SUB * share * HD * count, transcendentals=2 * REACH * SUB * share * count,
            bytes_accessed=6 * 2**20 * count // HEADS,
        ),
        name="attention",
    )(*operands)


def moved(block, step):
    devices = range(lax.axis_size("ctx"))
    route = [(i, step(i)) for i in devices if step(i) in devices]
    return lax.ppermute(block, "ctx", route)


def twin(block):
    return moved(block, lambda i: i ^ 1)


def ahead(block, chips):
    return moved(block, lambda i: i + 2 * chips)


def on_device(
    normed_input,
    frozen_query_output,
    key_base,
    frozen_value_output,
    out_grad,
    query_down_factor,
    query_up_factor,
    value_down_factor,
    value_up_factor,
    doc_lengths,
    stretch_map,
):
    devices = lax.axis_size("ctx")
    mine = lax.axis_index("ctx")
    chip, core = mine // 2, mine % 2
    stretch = stretch_map[mine]
    steps = jnp.arange(TOK, dtype=jnp.int32)
    places = stretch * TOK + steps
    documents = jnp.arange(doc_lengths.shape[0], dtype=jnp.int32)
    ends = jnp.sum(jnp.where(documents[:, None] >= documents[None, :], doc_lengths[None, :], 0), axis=1)
    starts = jnp.max(jnp.where(ends[None, :] <= places[:, None], ends[None, :], 0), axis=1)
    local = places - starts
    reach = 4 * TOK + steps - local
    half = HD // 2
    inverse = THETA ** (-jnp.arange(half, dtype=F32) * 2.0 / HD)
    angles = local.astype(F32)[:, None] * inverse[None, :]
    cosine, sine = jnp.cos(angles), jnp.sin(angles)
    cos = jnp.concatenate([cosine, cosine], axis=1)
    sin = jnp.concatenate([-sine, sine], axis=1)
    chips = chip - jnp.arange(3, dtype=jnp.int32)
    flips = (core + stretch_map[2 * jnp.maximum(chips, 0)]) % 2
    scalars = jnp.concatenate([(TOK * (1 - stretch % 2))[None], flips]).astype(jnp.int32)

    payloads = prepare(
        normed_input, query_down_factor.T, value_down_factor.T, key_base, frozen_value_output, value_up_factor, cos, sin
    )
    twins = [twin(payload) for payload in payloads]
    near = [ahead(payload, 1) for payload in payloads]
    far = [ahead(payload, 2) for payload in payloads]
    query = rotate_queries(frozen_query_output, payloads[0], query_up_factor, cos, sin)
    near[0], far[0], query = lax.optimization_barrier((near[0], far[0], query))
    lorad = held = None
    first = 0
    lift_q, lift_mine, lift_other = 0.0, 0.0, 0.0
    for place, count in enumerate(COUNTS):
        one, two = near[place], far[place]
        if held is not None:
            one, two, held[0] = lax.optimization_barrier((one, two, held[0]))
        window = [payloads[place], twins[place], one, twin(one), two, twin(two)]
        lorad = window if lorad is None else lorad
        *held, lq, lm, lo = attention(
            scalars, query, out_grad, payloads[0], query_up_factor, value_up_factor,
            cos, sin, reach[None, :], window, lorad, held, first, count,
        )
        first += count
        lift_q, lift_mine, lift_other = lift_q + lq, lift_mine + lm, lift_other + lo
    attended, key_mine, key_other, heads = held
    lift_q = (ADAPTER_SCALE * lift_q).astype(BF)
    lifts = lift_mine + twin(lift_other.astype(BF)).astype(F32)
    lift_near, lift_far = ahead(lifts[1].astype(BF), -1), ahead(lifts[2].astype(BF), -2)
    keyed = key_mine.astype(F32) + twin(key_other).astype(F32)
    own, one, two = keyed[0], keyed[1], keyed[2].astype(BF)
    lift_near, lift_far, own, one, two = lax.optimization_barrier((lift_near, lift_far, own, one, two))
    passed = ahead(two, -1)
    lift_v = lifts[0] + (lift_near.astype(F32) + lift_far.astype(F32))
    lift_v = (ADAPTER_SCALE * lift_v).astype(BF)
    kept, given = gradients(core[None], lift_q, lift_v, normed_input, heads)
    kept = (kept.astype(F32) + twin(given).astype(F32)).astype(BF)
    cores = [list(range(c, devices, 2)) for c in range(2)]
    spread = lax.all_to_all(kept, "ctx", 0, 0, axis_index_groups=cores, tiled=True)
    one = (one + passed.astype(F32)).astype(BF)
    key_total = own + ahead(one, -1).astype(F32)
    key_total = key_total.reshape(TOK, HEADS, HD)
    swapped = jnp.concatenate([key_total[..., half:], key_total[..., :half]], axis=-1)
    key_grad = (key_total * cos[:, None, :] - swapped * sin[:, None, :]).astype(BF).reshape(TOK, HEADS * HD)
    gathered = lax.all_to_all(sum_and_copy(spread), "ctx", 0, 0, axis_index_groups=cores, tiled=True)
    down_q, up_q, down_v, up_v = finish(core[None], gathered, twin(gathered), TOK * devices, normed_input.shape[1])
    return (attended, key_grad, down_q.T, up_q, down_v.T, up_v)


def solution(mesh):
    row = P("ctx", None)
    return jax.shard_map(
        on_device,
        mesh=mesh,
        in_specs=(row, row, row, row, row, P(), P(), P(), P(), P(), P()),
        out_specs=(row, row, P(), P(), P(), P()),
        check_vma=False,
    )
```

```python
import functools

import jax
import jax.numpy as jnp
from jax import lax
from jax.experimental import pallas as pl
from jax.experimental.pallas import tpu as pltpu
from jax.sharding import PartitionSpec as P

HD = 128
RANK = 64
TOK = 256
SUB = 128
REACH = 1152
SPANK = 5 * TOK
ROWS = 7 * TOK
KP = REACH
HEADS = 8
SHARE = 5
COUNTS = (3, 5)
UNIT = SHARE + 1
EDGE = UNIT * HEADS
VMEM_ASK = 60 * 2**20
THETA = 1000000.0
ADAPTER_SCALE = 2.0
LOG2E = 1.4426950408889634
NEG = -1e30
BF = jnp.bfloat16
F32 = jnp.float32


def mm(a, b):
    return lax.dot_general(a, b, (((1,), (0,)), ((), ())), preferred_element_type=F32)


def mm_nt(a, b):
    return lax.dot_general(a, b, (((1,), (1,)), ((), ())), preferred_element_type=F32)


def mm_tn(a, b):
    return lax.dot_general(a, b, (((0,), (0,)), ((), ())), preferred_element_type=F32)


def attention_kernel(share, first_call, sc, query, og, lora, qup, vup, cos, sin, dst, *rest):
    kin, vin, lin = rest[0:6], rest[6:12], rest[12:18]
    before_q, before_v = (None, None) if first_call else rest[18:20]
    rest = rest[18:] if first_call else rest[24:]
    att, dkm, dko, terms, liftq, lifts = rest[0:6]
    lvo = None if first_call else rest[6]
    rest = rest[6:] if first_call else rest[7:]
    kx, vx, kt, vt, lt, bias, ss, dka, dva, qn, dn, dnt, dqn, lva = rest
    g = pl.program_id(0)
    groups = pl.num_programs(0)
    wide = share * SUB
    scale = HD ** (-0.5)
    cexp = scale * LOG2E
    shift = pl.multiple_of(sc[0], TOK)

    def place(target, refs):
        for chip in range(3):
            low = pl.multiple_of((2 - chip) * 2 * TOK + shift, TOK)
            mine, other = refs[2 * chip], refs[2 * chip + 1]

            @pl.when(sc[1 + chip] == 0)
            def _():
                target[pl.ds(low, TOK), :] = mine[...]
                target[pl.ds(low + TOK, TOK), :] = other[...]

            @pl.when(sc[1 + chip] != 0)
            def _():
                target[pl.ds(low, TOK), :] = other[...]
                target[pl.ds(low + TOK, TOK), :] = mine[...]

    def take(read, mine, other):
        for chip in range(3):
            low = pl.multiple_of((2 - chip) * 2 * TOK + shift, TOK)

            @pl.when(sc[1 + chip] == 0)
            def _():
                mine[chip] = read(pl.ds(low, TOK)).astype(mine.dtype)
                other[chip] = read(pl.ds(low + TOK, TOK)).astype(other.dtype)

            @pl.when(sc[1 + chip] != 0)
            def _():
                mine[chip] = read(pl.ds(low + TOK, TOK)).astype(mine.dtype)
                other[chip] = read(pl.ds(low, TOK)).astype(other.dtype)

    @pl.when(g == 0)
    def _():
        for piece in (slice(0, TOK), slice(TOK + SPANK, ROWS)):
            dka[piece, :] = jnp.zeros((TOK, HD), F32)
            dva[piece, :] = jnp.zeros((TOK, HD), F32)
        if first_call:
            lva[...] = jnp.zeros_like(lva)
            liftq[...] = jnp.zeros_like(liftq)
        else:
            lva[...] = before_v[...]
            liftq[...] = before_q[...]
        place(kx, lin)
        lt[...] = kx[TOK : TOK + SPANK, :].T
        for b in range(2):
            first = dst[0:1, b * SUB : (b + 1) * SUB]
            last = SPANK - 2 * SUB + b * SUB + lax.broadcasted_iota(jnp.int32, (1, SUB), 1)
            key_at = b * SUB + lax.broadcasted_iota(jnp.int32, (REACH, SUB), 0)
            bias[b] = jnp.where((key_at >= first) & (key_at <= last), 0.0, NEG)

    place(kx, kin)
    place(vx, vin)
    kt[...] = kx[TOK : TOK + SPANK, :].T
    vt[...] = vx[TOK : TOK + SPANK, :].T
    for h in range(share):
        col = slice(h * HD, (h + 1) * HD)
        for b in range(2):
            qn[b, h * SUB : (h + 1) * SUB, :] = query[b * SUB : (b + 1) * SUB, col]
            dn[b, h * SUB : (h + 1) * SUB, :] = og[b * SUB : (b + 1) * SUB, col]
    pieces = [slice(i, i + KP) for i in range(0, REACH, KP)]

    keep = {}

    def phase_a(b):
        dnt[b] = dn[b].astype(F32).T
        query_t = qn[b].astype(F32).T.astype(BF)
        at = TOK + b * SUB
        top = None
        for piece in pieces:
            s = mm(kx[at + piece.start : at + piece.stop, :], query_t)
            s = s * cexp + jnp.concatenate([bias[b, piece, :]] * share, axis=1)
            ss[b, piece, :] = s
            t = jnp.max(s.reshape(KP // 8, 8, wide), axis=0)
            top = t if top is None else jnp.maximum(top, t)
        keep["top", b] = jnp.max(top, axis=0, keepdims=True)

    def phase_b(b):
        total = None
        for piece in pieces:
            e = jnp.exp2(ss[b, piece, :] - keep["top", b])
            t = jnp.sum(e.reshape(KP // 8, 8, wide), axis=0)
            total = t if total is None else total + t
        keep["norm", b] = keep["top", b] + jnp.log2(jnp.sum(total, axis=0, keepdims=True))

    def add(target, b, piece, value):
        rows = slice(TOK + b * SUB + piece.start, TOK + b * SUB + piece.stop)
        if b == 0:
            target[rows, :] = value
        elif piece.stop < REACH:
            target[rows, :] += value
        else:
            cut = KP - SUB
            target[rows.start : rows.start + cut, :] += value[:cut]
            target[rows.start + cut : rows.stop, :] = value[cut:]

    def phase_c(b):
        ot = None
        for piece in pieces:
            pb = jnp.exp2(ss[b, piece, :] - keep["norm", b]).astype(BF)
            t = mm(vt[:, b * SUB + piece.start : b * SUB + piece.stop], pb)
            ot = t if ot is None else ot + t
            add(dva, b, piece, mm(pb, dn[b]))
        ob = ot.astype(BF).astype(F32)
        keep["dot", b] = jnp.sum(dnt[b] * ob, axis=0, keepdims=True)
        obn = ob.T.astype(BF)
        for h in range(share):
            att[b * SUB : (b + 1) * SUB, h * HD : (h + 1) * HD] = obn[h * SUB : (h + 1) * SUB]

    def phase_d(b):
        qt = None
        grad_t = dnt[b].astype(BF)
        for piece in pieces:
            rows = slice(TOK + b * SUB + piece.start, TOK + b * SUB + piece.stop)
            p = jnp.exp2(ss[b, piece, :] - keep["norm", b])
            ds = (p * (mm(vx[rows, :], grad_t) - keep["dot", b])).astype(BF)
            t = mm(kt[:, b * SUB + piece.start : b * SUB + piece.stop], ds)
            qt = t if qt is None else qt + t
            add(dka, b, piece, mm(ds, qn[b]))
        dq = qt.T * scale
        rows = slice(b * SUB, (b + 1) * SUB)
        for h in range(share):
            u = dq[h * SUB : (h + 1) * SUB]
            dqn[rows, h * HD : (h + 1) * HD] = (
                u * cos[rows, :] - pltpu.roll(u, HD // 2, 1) * sin[rows, :]
            ).astype(BF)

    phase_a(0)
    phase_b(0)
    phase_a(1)
    phase_c(0)
    phase_b(1)
    phase_d(0)
    phase_c(1)
    phase_d(1)

    dqb = dqn[...]
    liftq[...] += mm_nt(dqb, qup[...])
    lora_t = lora[...].astype(F32).T[0:RANK].astype(BF)
    up = mm(lora_t, dqb)
    for h in range(share):
        terms[h] = (ADAPTER_SCALE * up[:, h * HD : (h + 1) * HD]).astype(BF)
    dvb = dva[TOK : TOK + SPANK, :].astype(BF)
    lva[TOK : TOK + SPANK, :] += mm_nt(dvb, vup[...])
    terms[share] = (ADAPTER_SCALE * mm(lt[...], dvb)[RANK : 2 * RANK]).astype(BF)
    take(lambda rows: (dka[rows, :] * scale).astype(BF), dkm, dko)

    @pl.when(g == groups - 1)
    def _():
        if first_call:
            lifts[...] = lva[...]
        else:
            take(lambda rows: lva[rows, :], lifts, lvo)


def prepare_kernel(normed, qdown, vdown, keys, values, vup, cos, sin, *outs):
    lora = mm_nt(normed[...], jnp.concatenate([qdown[...], vdown[...]], axis=0)).astype(BF)
    lora_v = lora[:, RANK:]
    head = 0
    for place, count in enumerate(COUNTS):
        out = outs[place]
        for c in range(count):
            col = slice((head + c) * HD, (head + c + 1) * HD)
            k = keys[:, col].astype(F32)
            k = k * cos[...] + pltpu.roll(k, HD // 2, 1) * sin[...]
            out[:, c * HD : (c + 1) * HD] = k.astype(BF)
            v = values[:, col].astype(F32) + ADAPTER_SCALE * mm(lora_v, vup[:, col])
            out[:, (count + c) * HD : (count + c + 1) * HD] = v.astype(BF)
        if place == 0:
            out[:, 2 * count * HD : (2 * count + 1) * HD] = lora
        head += count


def prepare(*operands):
    vmem = pl.BlockSpec(memory_space=pltpu.VMEM)
    widths = [2 * count * HD + (HD if place == 0 else 0) for place, count in enumerate(COUNTS)]
    return pl.pallas_call(
        prepare_kernel,
        out_shape=[jax.ShapeDtypeStruct((TOK, width), BF) for width in widths],
        in_specs=[vmem] * len(operands),
        out_specs=[vmem] * len(widths),
        compiler_params=pltpu.CompilerParams(vmem_limit_bytes=VMEM_ASK),
        name="prepare",
    )(*operands)


def rotate_kernel(frozen, lora, qup, cos, sin, query):
    extra = mm(lora[:, 0:RANK], qup[...])
    for h in range(SHARE):
        col = slice(h * HD, (h + 1) * HD)
        u = frozen[:, col].astype(F32) + ADAPTER_SCALE * extra[:, col]
        query[:, col] = (u * cos[...] + pltpu.roll(u, HD // 2, 1) * sin[...]).astype(BF)


def rotate_queries(frozen, own, qup, cos, sin):
    wide = SHARE * HD
    tail = 2 * COUNTS[0]
    table = pl.BlockSpec((TOK, HD), lambda g: (0, 0))
    return pl.pallas_call(
        rotate_kernel,
        out_shape=jax.ShapeDtypeStruct(frozen.shape, BF),
        grid=(HEADS,),
        in_specs=[
            pl.BlockSpec((TOK, wide), lambda g: (0, g)), pl.BlockSpec((TOK, HD), lambda g: (0, tail)),
            pl.BlockSpec((RANK, wide), lambda g: (0, g)), table, table,
        ],
        out_specs=pl.BlockSpec((TOK, wide), lambda g: (0, g)),
        compiler_params=pltpu.CompilerParams(vmem_limit_bytes=VMEM_ASK),
        name="rotate_queries",
    )(frozen, own, qup, cos, sin)


def gradients_kernel(core, total_q, own, near, far, normed, heads, kept, given):
    lift_q = (ADAPTER_SCALE * total_q[...]).astype(BF)
    lift_v = own[...] + (near[...].astype(F32) + far[...].astype(F32))
    lift_v = (ADAPTER_SCALE * lift_v).astype(BF)
    down = mm_tn(jnp.concatenate([lift_q, lift_v], axis=1), normed[...]).astype(BF)
    tiles = down.shape[1] // HD

    def write(low, high):
        for place, out in enumerate((low, high)):
            out[0 : EDGE // 2] = heads[place * EDGE // 2 : (place + 1) * EDGE // 2]
            for i in range(tiles // 2):
                col = slice((place * tiles // 2 + i) * HD, (place * tiles // 2 + i + 1) * HD)
                out[EDGE // 2 + i] = down[:RANK, col]
                out[EDGE // 2 + tiles // 2 + i] = down[RANK:, col]

    @pl.when(core[0] == 0)
    def _():
        write(kept, given)

    @pl.when(core[0] != 0)
    def _():
        write(given, kept)


def gradients(core, total_q, own, near, far, normed, heads):
    vmem = pl.BlockSpec(memory_space=pltpu.VMEM)
    half = jax.ShapeDtypeStruct((EDGE // 2 + normed.shape[1] // HD, RANK, HD), BF)
    return pl.pallas_call(
        gradients_kernel,
        out_shape=[half, half],
        in_specs=[pl.BlockSpec(memory_space=pltpu.SMEM)] + [vmem] * 6,
        out_specs=[vmem] * 2,
        compiler_params=pltpu.CompilerParams(vmem_limit_bytes=24 * 2**20),
        name="gradients",
    )(core, total_q, own, near, far, normed, heads)


def sum_kernel(spread, out):
    total = jnp.zeros(out.shape[1:], F32)
    for i in range(spread.shape[0]):
        total = total + spread[i].astype(F32)
    low = total.astype(BF)
    for i in range(spread.shape[0]):
        out[i] = low


def sum_and_copy(spread):
    vmem = pl.BlockSpec(memory_space=pltpu.VMEM)
    return pl.pallas_call(
        sum_kernel, out_shape=jax.ShapeDtypeStruct(spread.shape, BF), in_specs=[vmem], out_specs=vmem, name="sum_and_copy"
    )(spread)


def finish_kernel(scale, core, mine, other, down_q, up_q, down_v, up_v):
    def write(low, high):
        for place, half in enumerate((low, high)):
            for i in range(HEADS // 2):
                h = place * HEADS // 2 + i
                for c in range(SHARE):
                    at = (h * SHARE + c) * HD
                    up_q[:, at : at + HD] = half[i * UNIT + c].astype(F32) * scale
                up_v[:, h * HD : (h + 1) * HD] = half[i * UNIT + SHARE].astype(F32) * scale
            tiles = down_q.shape[1] // HD // 2
            for i in range(tiles):
                col = slice((place * tiles + i) * HD, (place * tiles + i + 1) * HD)
                down_q[:, col] = half[EDGE // 2 + i].astype(F32) * scale
                down_v[:, col] = half[EDGE // 2 + tiles + i].astype(F32) * scale

    @pl.when(core[0] == 0)
    def _():
        write(mine, other)

    @pl.when(core[0] != 0)
    def _():
        write(other, mine)


def finish(core, mine, other, tokens, width):
    vmem = pl.BlockSpec(memory_space=pltpu.VMEM)
    query = jax.ShapeDtypeStruct((RANK, HEADS * SHARE * HD), F32)
    down = jax.ShapeDtypeStruct((RANK, width), F32)
    value = jax.ShapeDtypeStruct((RANK, HEADS * HD), F32)
    return pl.pallas_call(
        functools.partial(finish_kernel, 1.0 / tokens),
        out_shape=[down, query, down, value],
        in_specs=[pl.BlockSpec(memory_space=pltpu.SMEM), vmem, vmem],
        out_specs=[vmem] * 4,
        compiler_params=pltpu.CompilerParams(vmem_limit_bytes=VMEM_ASK),
        name="finish",
    )(core, mine, other)


def attention(scalars, query, grad, own, qup, vup, cos, sin, dst, keyed, lorad, held, lifts, first, count):
    share = SHARE
    wide = share * HD
    tail = 2 * COUNTS[0]

    def whole(shape):
        return pl.BlockSpec(shape, lambda g, s: (0,) * len(shape))

    def column(rows, width, offset):
        return pl.BlockSpec((rows, width), lambda g, s: (0, g + offset))

    lora_spec = pl.BlockSpec((TOK, HD), lambda g, s: (0, tail))
    in_specs = [
        column(TOK, wide, first), column(TOK, wide, first), lora_spec,
        column(RANK, wide, first), column(RANK, HD, first),
        whole((TOK, HD)), whole((TOK, HD)), whole((1, TOK)),
    ]
    in_specs += [column(TOK, HD, 0)] * 6 + [column(TOK, HD, count)] * 6 + [lora_spec] * 6
    operands = [scalars, query, grad, own, qup, vup, cos, sin, dst, *keyed, *keyed, *lorad]
    aliases = {}
    if held is not None:
        operands += lifts
        in_specs += [whole((TOK, RANK)), whole((ROWS, RANK))]
        aliases = {len(operands) + i: i for i in range(len(held))}
        operands += held
        in_specs += [pl.BlockSpec(memory_space=pl.ANY)] * len(held)
    pair = jax.ShapeDtypeStruct((3, TOK, HEADS * HD), BF)
    lift = (3, TOK, RANK)
    out_shape = [
        jax.ShapeDtypeStruct(query.shape, BF), pair, pair, jax.ShapeDtypeStruct((EDGE, RANK, HD), BF),
        jax.ShapeDtypeStruct((TOK, RANK), F32),
    ]
    if held is None:
        out_shape += [jax.ShapeDtypeStruct((ROWS, RANK), F32)]
        lift_specs = [whole((ROWS, RANK))]
    else:
        out_shape += [jax.ShapeDtypeStruct(lift, F32), jax.ShapeDtypeStruct(lift, BF)]
        lift_specs = [whole(lift)] * 2
    pair_spec = pl.BlockSpec((3, TOK, HD), lambda g, s: (0, 0, g + first))
    out_specs = [
        column(TOK, wide, first), pair_spec, pair_spec,
        pl.BlockSpec((UNIT, RANK, HD), lambda g, s: (g + first, 0, 0)),
        whole((TOK, RANK)), *lift_specs,
    ]
    wide_rows = share * SUB
    scratch = [
        pltpu.VMEM((ROWS, HD), BF), pltpu.VMEM((ROWS, HD), BF),
        pltpu.VMEM((HD, SPANK), BF), pltpu.VMEM((HD, SPANK), BF), pltpu.VMEM((HD, SPANK), BF),
        pltpu.VMEM((2, REACH, SUB), F32),
        pltpu.VMEM((2, REACH, wide_rows), F32),
        pltpu.VMEM((ROWS, HD), F32), pltpu.VMEM((ROWS, HD), F32),
        pltpu.VMEM((2, wide_rows, HD), BF), pltpu.VMEM((2, wide_rows, HD), BF),
        pltpu.VMEM((2, HD, wide_rows), F32), pltpu.VMEM((TOK, wide), BF),
        pltpu.VMEM((ROWS, RANK), F32),
    ]
    return pl.pallas_call(
        functools.partial(attention_kernel, share, held is None),
        out_shape=out_shape,
        grid_spec=pltpu.PrefetchScalarGridSpec(
            num_scalar_prefetch=1, grid=(count,), in_specs=in_specs, out_specs=out_specs, scratch_shapes=scratch
        ),
        input_output_aliases=aliases,
        compiler_params=pltpu.CompilerParams(
            dimension_semantics=("arbitrary",), vmem_limit_bytes=VMEM_ASK
        ),
        cost_estimate=pl.CostEstimate(
            flops=12 * 2 * REACH * SUB * share * HD * count, transcendentals=2 * REACH * SUB * share * count,
            bytes_accessed=6 * 2**20 * count // HEADS,
        ),
        name="attention",
    )(*operands)


def moved(block, step):
    devices = range(lax.axis_size("ctx"))
    route = [(i, step(i)) for i in devices if step(i) in devices]
    return lax.ppermute(block, "ctx", route)


def twin(block):
    return moved(block, lambda i: i ^ 1)


def ahead(block, chips):
    return moved(block, lambda i: i + 2 * chips)


def on_device(
    normed_input,
    frozen_query_output,
    key_base,
    frozen_value_output,
    out_grad,
    query_down_factor,
    query_up_factor,
    value_down_factor,
    value_up_factor,
    doc_lengths,
    stretch_map,
):
    devices = lax.axis_size("ctx")
    mine = lax.axis_index("ctx")
    chip, core = mine // 2, mine % 2
    stretch = stretch_map[mine]
    steps = jnp.arange(TOK, dtype=jnp.int32)
    places = stretch * TOK + steps
    documents = jnp.arange(doc_lengths.shape[0], dtype=jnp.int32)
    ends = jnp.sum(jnp.where(documents[:, None] >= documents[None, :], doc_lengths[None, :], 0), axis=1)
    starts = jnp.max(jnp.where(ends[None, :] <= places[:, None], ends[None, :], 0), axis=1)
    local = places - starts
    reach = 4 * TOK + steps - local
    half = HD // 2
    inverse = THETA ** (-jnp.arange(half, dtype=F32) * 2.0 / HD)
    angles = local.astype(F32)[:, None] * inverse[None, :]
    cosine, sine = jnp.cos(angles), jnp.sin(angles)
    cos = jnp.concatenate([cosine, cosine], axis=1)
    sin = jnp.concatenate([-sine, sine], axis=1)
    chips = chip - jnp.arange(3, dtype=jnp.int32)
    flips = (core + stretch_map[2 * jnp.maximum(chips, 0)]) % 2
    scalars = jnp.concatenate([(TOK * (1 - stretch % 2))[None], flips]).astype(jnp.int32)

    payloads = prepare(
        normed_input, query_down_factor.T, value_down_factor.T, key_base, frozen_value_output, value_up_factor, cos, sin
    )
    twins = [twin(payload) for payload in payloads]
    near = [ahead(payload, 1) for payload in payloads]
    far = [ahead(payload, 2) for payload in payloads]
    query = rotate_queries(frozen_query_output, payloads[0], query_up_factor, cos, sin)
    near[0], far[0], query = lax.optimization_barrier((near[0], far[0], query))
    lorad = held = lifts = None
    first = 0
    for place, count in enumerate(COUNTS):
        one, two = near[place], far[place]
        if held is not None:
            one, two, held[0] = lax.optimization_barrier((one, two, held[0]))
        window = [payloads[place], twins[place], one, twin(one), two, twin(two)]
        lorad = window if lorad is None else lorad
        results = attention(
            scalars, query, out_grad, payloads[0], query_up_factor, value_up_factor,
            cos, sin, reach[None, :], window, lorad, held, lifts, first, count,
        )
        held, lifts = list(results[:4]), list(results[4:])
        first += count
    attended, key_mine, key_other, heads = held
    lift_q, lift_mine, lift_other = lifts
    lifts = lift_mine + twin(lift_other).astype(F32)
    lift_near, lift_far = ahead(lifts[1].astype(BF), -1), ahead(lifts[2].astype(BF), -2)
    keyed = key_mine.astype(F32) + twin(key_other).astype(F32)
    own, one, two = keyed[0], keyed[1], keyed[2].astype(BF)
    lift_near, lift_far, own, one, two = lax.optimization_barrier((lift_near, lift_far, own, one, two))
    passed = ahead(two, -1)
    kept, given = gradients(core[None], lift_q, lifts[0], lift_near, lift_far, normed_input, heads)
    kept = (kept.astype(F32) + twin(given).astype(F32)).astype(BF)
    cores = [list(range(c, devices, 2)) for c in range(2)]
    spread = lax.all_to_all(kept, "ctx", 0, 0, axis_index_groups=cores, tiled=True)
    one = (one + passed.astype(F32)).astype(BF)
    last = ahead(one, -1)
    gathered = lax.all_to_all(sum_and_copy(spread), "ctx", 0, 0, axis_index_groups=cores, tiled=True)
    sums = finish(core[None], gathered, twin(gathered), TOK * devices, normed_input.shape[1])
    key_total = (own + last.astype(F32)).reshape(TOK, HEADS, HD)
    swapped = jnp.concatenate([key_total[..., half:], key_total[..., :half]], axis=-1)
    key_grad = (key_total * cos[:, None, :] - swapped * sin[:, None, :]).astype(BF).reshape(TOK, HEADS * HD)
    down_q, up_q, down_v, up_v = sums
    return (attended, key_grad, down_q.T, up_q, down_v.T, up_v)


def solution(mesh):
    row = P("ctx", None)
    return jax.shard_map(
        on_device,
        mesh=mesh,
        in_specs=(row, row, row, row, row, P(), P(), P(), P(), P(), P()),
        out_specs=(row, row, P(), P(), P(), P()),
        check_vma=False,
    )
```

```python
import functools

import jax
import jax.numpy as jnp
from jax import lax
from jax.experimental import pallas as pl
from jax.experimental.pallas import tpu as pltpu
from jax.sharding import PartitionSpec as P

HD = 128
RANK = 64
TOK = 256
SUB = 128
REACH = 1152
SPANK = 5 * TOK
ROWS = 7 * TOK
KP = REACH
HEADS = 8
SHARE = 5
COUNTS = (3, 5)
UNIT = SHARE + 1
EDGE = UNIT * HEADS
VMEM_ASK = 60 * 2**20
THETA = 1000000.0
ADAPTER_SCALE = 2.0
LOG2E = 1.4426950408889634
NEG = -1e30
BF = jnp.bfloat16
F32 = jnp.float32


def mm(a, b):
    return lax.dot_general(a, b, (((1,), (0,)), ((), ())), preferred_element_type=F32)


def mm_nt(a, b):
    return lax.dot_general(a, b, (((1,), (1,)), ((), ())), preferred_element_type=F32)


def mm_tn(a, b):
    return lax.dot_general(a, b, (((0,), (0,)), ((), ())), preferred_element_type=F32)


def attention_kernel(share, first_call, sc, query, og, lora, qup, vup, cos, sin, dst, *rest):
    kin, vin, lin = rest[0:6], rest[6:12], rest[12:18]
    before_q, before_v = (None, None) if first_call else rest[18:20]
    rest = rest[18:] if first_call else rest[24:]
    att, dkm, dko, terms, liftq, lifts = rest[0:6]
    lvo = None if first_call else rest[6]
    rest = rest[6:] if first_call else rest[7:]
    kx, vx, kt, vt, lt, bias, ss, dka, dva, qn, dn, dnt, dqn, lva = rest
    g = pl.program_id(0)
    groups = pl.num_programs(0)
    wide = share * SUB
    scale = HD ** (-0.5)
    cexp = scale * LOG2E
    shift = pl.multiple_of(sc[0], TOK)

    def place(target, refs):
        for chip in range(3):
            low = pl.multiple_of((2 - chip) * 2 * TOK + shift, TOK)
            mine, other = refs[2 * chip], refs[2 * chip + 1]

            @pl.when(sc[1 + chip] == 0)
            def _():
                target[pl.ds(low, TOK), :] = mine[...]
                target[pl.ds(low + TOK, TOK), :] = other[...]

            @pl.when(sc[1 + chip] != 0)
            def _():
                target[pl.ds(low, TOK), :] = other[...]
                target[pl.ds(low + TOK, TOK), :] = mine[...]

    def take(read, mine, other):
        for chip in range(3):
            low = pl.multiple_of((2 - chip) * 2 * TOK + shift, TOK)

            @pl.when(sc[1 + chip] == 0)
            def _():
                mine[chip] = read(pl.ds(low, TOK)).astype(mine.dtype)
                other[chip] = read(pl.ds(low + TOK, TOK)).astype(other.dtype)

            @pl.when(sc[1 + chip] != 0)
            def _():
                mine[chip] = read(pl.ds(low + TOK, TOK)).astype(mine.dtype)
                other[chip] = read(pl.ds(low, TOK)).astype(other.dtype)

    @pl.when(g == 0)
    def _():
        for piece in (slice(0, TOK), slice(TOK + SPANK, ROWS)):
            dka[piece, :] = jnp.zeros((TOK, HD), F32)
            dva[piece, :] = jnp.zeros((TOK, HD), F32)
        if first_call:
            lva[...] = jnp.zeros_like(lva)
            liftq[...] = jnp.zeros_like(liftq)
        else:
            lva[...] = before_v[...]
            liftq[...] = before_q[...]
        place(kx, lin)
        lt[...] = kx[TOK : TOK + SPANK, :].T
        for b in range(2):
            first = dst[0:1, b * SUB : (b + 1) * SUB]
            last = SPANK - 2 * SUB + b * SUB + lax.broadcasted_iota(jnp.int32, (1, SUB), 1)
            key_at = b * SUB + lax.broadcasted_iota(jnp.int32, (REACH, SUB), 0)
            bias[b] = jnp.where((key_at >= first) & (key_at <= last), 0.0, NEG)

    place(kx, kin)
    place(vx, vin)
    kt[...] = kx[TOK : TOK + SPANK, :].T
    vt[...] = vx[TOK : TOK + SPANK, :].T
    for h in range(share):
        col = slice(h * HD, (h + 1) * HD)
        for b in range(2):
            qn[b, h * SUB : (h + 1) * SUB, :] = query[b * SUB : (b + 1) * SUB, col]
            dn[b, h * SUB : (h + 1) * SUB, :] = og[b * SUB : (b + 1) * SUB, col]
    pieces = [slice(i, i + KP) for i in range(0, REACH, KP)]

    keep = {}

    def phase_a(b):
        dnt[b] = dn[b].astype(F32).T
        query_t = qn[b].astype(F32).T.astype(BF)
        at = TOK + b * SUB
        top = None
        for piece in pieces:
            s = mm(kx[at + piece.start : at + piece.stop, :], query_t)
            s = s * cexp + jnp.concatenate([bias[b, piece, :]] * share, axis=1)
            ss[b, piece, :] = s
            t = jnp.max(s.reshape(KP // 8, 8, wide), axis=0)
            top = t if top is None else jnp.maximum(top, t)
        keep["top", b] = jnp.max(top, axis=0, keepdims=True)

    def phase_b(b):
        total = None
        for piece in pieces:
            e = jnp.exp2(ss[b, piece, :] - keep["top", b])
            t = jnp.sum(e.reshape(KP // 8, 8, wide), axis=0)
            total = t if total is None else total + t
        keep["norm", b] = keep["top", b] + jnp.log2(jnp.sum(total, axis=0, keepdims=True))

    def add(target, b, piece, value):
        rows = slice(TOK + b * SUB + piece.start, TOK + b * SUB + piece.stop)
        if b == 0:
            target[rows, :] = value
        elif piece.stop < REACH:
            target[rows, :] += value
        else:
            cut = KP - SUB
            target[rows.start : rows.start + cut, :] += value[:cut]
            target[rows.start + cut : rows.stop, :] = value[cut:]

    def phase_c(b):
        ot = None
        for piece in pieces:
            pb = jnp.exp2(ss[b, piece, :] - keep["norm", b]).astype(BF)
            t = mm(vt[:, b * SUB + piece.start : b * SUB + piece.stop], pb)
            ot = t if ot is None else ot + t
            add(dva, b, piece, mm(pb, dn[b]))
        ob = ot.astype(BF).astype(F32)
        keep["dot", b] = jnp.sum(dnt[b] * ob, axis=0, keepdims=True)
        obn = ob.T.astype(BF)
        for h in range(share):
            att[b * SUB : (b + 1) * SUB, h * HD : (h + 1) * HD] = obn[h * SUB : (h + 1) * SUB]

    def phase_d(b):
        qt = None
        grad_t = dnt[b].astype(BF)
        for piece in pieces:
            rows = slice(TOK + b * SUB + piece.start, TOK + b * SUB + piece.stop)
            p = jnp.exp2(ss[b, piece, :] - keep["norm", b])
            ds = (p * (mm(vx[rows, :], grad_t) - keep["dot", b])).astype(BF)
            t = mm(kt[:, b * SUB + piece.start : b * SUB + piece.stop], ds)
            qt = t if qt is None else qt + t
            add(dka, b, piece, mm(ds, qn[b]))
        dq = qt.T * scale
        rows = slice(b * SUB, (b + 1) * SUB)
        for h in range(share):
            u = dq[h * SUB : (h + 1) * SUB]
            dqn[rows, h * HD : (h + 1) * HD] = (
                u * cos[rows, :] - pltpu.roll(u, HD // 2, 1) * sin[rows, :]
            ).astype(BF)

    phase_a(0)
    phase_b(0)
    phase_a(1)
    phase_c(0)
    phase_b(1)
    phase_d(0)
    phase_c(1)
    phase_d(1)

    dqb = dqn[...]
    liftq[...] += mm_nt(dqb, qup[...])
    lora_t = lora[...].astype(F32).T[0:RANK].astype(BF)
    up = mm(lora_t, dqb)
    for h in range(share):
        terms[h] = (ADAPTER_SCALE * up[:, h * HD : (h + 1) * HD]).astype(BF)
    dvb = dva[TOK : TOK + SPANK, :].astype(BF)
    lva[TOK : TOK + SPANK, :] += mm_nt(dvb, vup[...])
    terms[share] = (ADAPTER_SCALE * mm(lt[...], dvb)[RANK : 2 * RANK]).astype(BF)
    take(lambda rows: (dka[rows, :] * scale).astype(BF), dkm, dko)

    @pl.when(g == groups - 1)
    def _():
        if first_call:
            lifts[...] = lva[...]
        else:
            take(lambda rows: lva[rows, :], lifts, lvo)


def prepare_kernel(normed, qdown, vdown, keys, values, vup, cos, sin, *outs):
    lora = mm_nt(normed[...], jnp.concatenate([qdown[...], vdown[...]], axis=0)).astype(BF)
    lora_v = lora[:, RANK:]
    head = 0
    for place, count in enumerate(COUNTS):
        out = outs[place]
        for c in range(count):
            col = slice((head + c) * HD, (head + c + 1) * HD)
            k = keys[:, col].astype(F32)
            k = k * cos[...] + pltpu.roll(k, HD // 2, 1) * sin[...]
            out[:, c * HD : (c + 1) * HD] = k.astype(BF)
            v = values[:, col].astype(F32) + ADAPTER_SCALE * mm(lora_v, vup[:, col])
            out[:, (count + c) * HD : (count + c + 1) * HD] = v.astype(BF)
        if place == 0:
            out[:, 2 * count * HD : (2 * count + 1) * HD] = lora
        head += count


def prepare(*operands):
    vmem = pl.BlockSpec(memory_space=pltpu.VMEM)
    widths = [2 * count * HD + (HD if place == 0 else 0) for place, count in enumerate(COUNTS)]
    return pl.pallas_call(
        prepare_kernel,
        out_shape=[jax.ShapeDtypeStruct((TOK, width), BF) for width in widths],
        in_specs=[vmem] * len(operands),
        out_specs=[vmem] * len(widths),
        compiler_params=pltpu.CompilerParams(vmem_limit_bytes=VMEM_ASK),
        name="prepare",
    )(*operands)


def rotate_kernel(frozen, lora, qup, cos, sin, query):
    extra = mm(lora[:, 0:RANK], qup[...])
    for h in range(SHARE):
        col = slice(h * HD, (h + 1) * HD)
        u = frozen[:, col].astype(F32) + ADAPTER_SCALE * extra[:, col]
        query[:, col] = (u * cos[...] + pltpu.roll(u, HD // 2, 1) * sin[...]).astype(BF)


def rotate_queries(frozen, own, qup, cos, sin):
    wide = SHARE * HD
    tail = 2 * COUNTS[0]
    table = pl.BlockSpec((TOK, HD), lambda g: (0, 0))
    return pl.pallas_call(
        rotate_kernel,
        out_shape=jax.ShapeDtypeStruct(frozen.shape, BF),
        grid=(HEADS,),
        in_specs=[
            pl.BlockSpec((TOK, wide), lambda g: (0, g)), pl.BlockSpec((TOK, HD), lambda g: (0, tail)),
            pl.BlockSpec((RANK, wide), lambda g: (0, g)), table, table,
        ],
        out_specs=pl.BlockSpec((TOK, wide), lambda g: (0, g)),
        compiler_params=pltpu.CompilerParams(vmem_limit_bytes=VMEM_ASK),
        name="rotate_queries",
    )(frozen, own, qup, cos, sin)


def gradients_kernel(core, total_q, own, near, far, normed, heads, kept, given):
    lift_q = (ADAPTER_SCALE * total_q[...]).astype(BF)
    lift_v = own[...] + (near[...].astype(F32) + far[...].astype(F32))
    lift_v = (ADAPTER_SCALE * lift_v).astype(BF)
    down = mm_tn(jnp.concatenate([lift_q, lift_v], axis=1), normed[...]).astype(BF)
    tiles = down.shape[1] // HD

    def write(low, high):
        for place, out in enumerate((low, high)):
            out[0 : EDGE // 2] = heads[place * EDGE // 2 : (place + 1) * EDGE // 2]
            for i in range(tiles // 2):
                col = slice((place * tiles // 2 + i) * HD, (place * tiles // 2 + i + 1) * HD)
                out[EDGE // 2 + i] = down[:RANK, col]
                out[EDGE // 2 + tiles // 2 + i] = down[RANK:, col]

    @pl.when(core[0] == 0)
    def _():
        write(kept, given)

    @pl.when(core[0] != 0)
    def _():
        write(given, kept)


def gradients(core, total_q, own, near, far, normed, heads):
    vmem = pl.BlockSpec(memory_space=pltpu.VMEM)
    half = jax.ShapeDtypeStruct((EDGE // 2 + normed.shape[1] // HD, RANK, HD), BF)
    return pl.pallas_call(
        gradients_kernel,
        out_shape=[half, half],
        in_specs=[pl.BlockSpec(memory_space=pltpu.SMEM)] + [vmem] * 6,
        out_specs=[vmem] * 2,
        compiler_params=pltpu.CompilerParams(vmem_limit_bytes=24 * 2**20),
        name="gradients",
    )(core, total_q, own, near, far, normed, heads)


def sum_kernel(spread, out):
    total = jnp.zeros(out.shape[1:], F32)
    for i in range(spread.shape[0]):
        total = total + spread[i].astype(F32)
    low = total.astype(BF)
    for i in range(spread.shape[0]):
        out[i] = low


def sum_and_copy(spread):
    vmem = pl.BlockSpec(memory_space=pltpu.VMEM)
    return pl.pallas_call(
        sum_kernel, out_shape=jax.ShapeDtypeStruct(spread.shape, BF), in_specs=[vmem], out_specs=vmem, name="sum_and_copy"
    )(spread)


def finish_kernel(scale, core, mine, other, down_q, up_q, down_v, up_v):
    def write(low, high):
        for place, half in enumerate((low, high)):
            for i in range(HEADS // 2):
                h = place * HEADS // 2 + i
                for c in range(SHARE):
                    at = (h * SHARE + c) * HD
                    up_q[:, at : at + HD] = half[i * UNIT + c].astype(F32) * scale
                up_v[:, h * HD : (h + 1) * HD] = half[i * UNIT + SHARE].astype(F32) * scale
            tiles = down_q.shape[1] // HD // 2
            for i in range(tiles):
                col = slice((place * tiles + i) * HD, (place * tiles + i + 1) * HD)
                down_q[:, col] = half[EDGE // 2 + i].astype(F32) * scale
                down_v[:, col] = half[EDGE // 2 + tiles + i].astype(F32) * scale

    @pl.when(core[0] == 0)
    def _():
        write(mine, other)

    @pl.when(core[0] != 0)
    def _():
        write(other, mine)


def finish(core, mine, other, tokens, width):
    vmem = pl.BlockSpec(memory_space=pltpu.VMEM)
    query = jax.ShapeDtypeStruct((RANK, HEADS * SHARE * HD), F32)
    down = jax.ShapeDtypeStruct((RANK, width), F32)
    value = jax.ShapeDtypeStruct((RANK, HEADS * HD), F32)
    return pl.pallas_call(
        functools.partial(finish_kernel, 1.0 / tokens),
        out_shape=[down, query, down, value],
        in_specs=[pl.BlockSpec(memory_space=pltpu.SMEM), vmem, vmem],
        out_specs=[vmem] * 4,
        compiler_params=pltpu.CompilerParams(vmem_limit_bytes=VMEM_ASK),
        name="finish",
    )(core, mine, other)


def attention(scalars, query, grad, own, qup, vup, cos, sin, dst, keyed, lorad, held, lifts, first, count):
    share = SHARE
    wide = share * HD
    tail = 2 * COUNTS[0]

    def whole(shape):
        return pl.BlockSpec(shape, lambda g, s: (0,) * len(shape))

    def column(rows, width, offset):
        return pl.BlockSpec((rows, width), lambda g, s: (0, g + offset))

    lora_spec = pl.BlockSpec((TOK, HD), lambda g, s: (0, tail))
    in_specs = [
        column(TOK, wide, first), column(TOK, wide, first), lora_spec,
        column(RANK, wide, first), column(RANK, HD, first),
        whole((TOK, HD)), whole((TOK, HD)), whole((1, TOK)),
    ]
    in_specs += [column(TOK, HD, 0)] * 6 + [column(TOK, HD, count)] * 6 + [lora_spec] * 6
    operands = [scalars, query, grad, own, qup, vup, cos, sin, dst, *keyed, *keyed, *lorad]
    aliases = {}
    if held is not None:
        operands += lifts
        in_specs += [whole((TOK, RANK)), whole((ROWS, RANK))]
        aliases = {len(operands) + i: i for i in range(len(held))}
        operands += held
        in_specs += [pl.BlockSpec(memory_space=pl.ANY)] * len(held)
    pair = jax.ShapeDtypeStruct((3, TOK, HEADS * HD), BF)
    lift = (3, TOK, RANK)
    out_shape = [
        jax.ShapeDtypeStruct(query.shape, BF), pair, pair, jax.ShapeDtypeStruct((EDGE, RANK, HD), BF),
        jax.ShapeDtypeStruct((TOK, RANK), F32),
    ]
    if held is None:
        out_shape += [jax.ShapeDtypeStruct((ROWS, RANK), F32)]
        lift_specs = [whole((ROWS, RANK))]
    else:
        out_shape += [jax.ShapeDtypeStruct(lift, F32), jax.ShapeDtypeStruct(lift, BF)]
        lift_specs = [whole(lift)] * 2
    pair_spec = pl.BlockSpec((3, TOK, HD), lambda g, s: (0, 0, g + first))
    out_specs = [
        column(TOK, wide, first), pair_spec, pair_spec,
        pl.BlockSpec((UNIT, RANK, HD), lambda g, s: (g + first, 0, 0)),
        whole((TOK, RANK)), *lift_specs,
    ]
    wide_rows = share * SUB
    scratch = [
        pltpu.VMEM((ROWS, HD), BF), pltpu.VMEM((ROWS, HD), BF),
        pltpu.VMEM((HD, SPANK), BF), pltpu.VMEM((HD, SPANK), BF), pltpu.VMEM((HD, SPANK), BF),
        pltpu.VMEM((2, REACH, SUB), F32),
        pltpu.VMEM((2, REACH, wide_rows), F32),
        pltpu.VMEM((ROWS, HD), F32), pltpu.VMEM((ROWS, HD), F32),
        pltpu.VMEM((2, wide_rows, HD), BF), pltpu.VMEM((2, wide_rows, HD), BF),
        pltpu.VMEM((2, HD, wide_rows), F32), pltpu.VMEM((TOK, wide), BF),
        pltpu.VMEM((ROWS, RANK), F32),
    ]
    return pl.pallas_call(
        functools.partial(attention_kernel, share, held is None),
        out_shape=out_shape,
        grid_spec=pltpu.PrefetchScalarGridSpec(
            num_scalar_prefetch=1, grid=(count,), in_specs=in_specs, out_specs=out_specs, scratch_shapes=scratch
        ),
        input_output_aliases=aliases,
        compiler_params=pltpu.CompilerParams(
            dimension_semantics=("arbitrary",), vmem_limit_bytes=VMEM_ASK
        ),
        cost_estimate=pl.CostEstimate(
            flops=12 * 2 * REACH * SUB * share * HD * count, transcendentals=2 * REACH * SUB * share * count,
            bytes_accessed=6 * 2**20 * count // HEADS,
        ),
        name="attention",
    )(*operands)


def moved(block, step):
    devices = range(lax.axis_size("ctx"))
    route = [(i, step(i)) for i in devices if step(i) in devices]
    return lax.ppermute(block, "ctx", route)


def twin(block):
    return moved(block, lambda i: i ^ 1)


def ahead(block, chips):
    return moved(block, lambda i: i + 2 * chips)


def on_device(
    normed_input,
    frozen_query_output,
    key_base,
    frozen_value_output,
    out_grad,
    query_down_factor,
    query_up_factor,
    value_down_factor,
    value_up_factor,
    doc_lengths,
    stretch_map,
):
    devices = lax.axis_size("ctx")
    mine = lax.axis_index("ctx")
    chip, core = mine // 2, mine % 2
    stretch = stretch_map[mine]
    steps = jnp.arange(TOK, dtype=jnp.int32)
    places = stretch * TOK + steps
    documents = jnp.arange(doc_lengths.shape[0], dtype=jnp.int32)
    ends = jnp.sum(jnp.where(documents[:, None] >= documents[None, :], doc_lengths[None, :], 0), axis=1)
    starts = jnp.max(jnp.where(ends[None, :] <= places[:, None], ends[None, :], 0), axis=1)
    local = places - starts
    reach = 4 * TOK + steps - local
    half = HD // 2
    inverse = THETA ** (-jnp.arange(half, dtype=F32) * 2.0 / HD)
    angles = local.astype(F32)[:, None] * inverse[None, :]
    cosine, sine = jnp.cos(angles), jnp.sin(angles)
    cos = jnp.concatenate([cosine, cosine], axis=1)
    sin = jnp.concatenate([-sine, sine], axis=1)
    chips = chip - jnp.arange(3, dtype=jnp.int32)
    flips = (core + stretch_map[2 * jnp.maximum(chips, 0)]) % 2
    scalars = jnp.concatenate([(TOK * (1 - stretch % 2))[None], flips]).astype(jnp.int32)

    payloads = prepare(
        normed_input, query_down_factor.T, value_down_factor.T, key_base, frozen_value_output, value_up_factor, cos, sin
    )
    twins = [twin(payload) for payload in payloads]
    near = [ahead(payload, 1) for payload in payloads]
    far = [ahead(payload, 2) for payload in payloads]
    query = rotate_queries(frozen_query_output, payloads[0], query_up_factor, cos, sin)
    near[0], far[0], query = lax.optimization_barrier((near[0], far[0], query))
    lorad = held = lifts = None
    first = 0
    for place, count in enumerate(COUNTS):
        one, two = near[place], far[place]
        if held is not None:
            one, two, held[0] = lax.optimization_barrier((one, two, held[0]))
        window = [payloads[place], twins[place], one, twin(one), two, twin(two)]
        lorad = window if lorad is None else lorad
        results = attention(
            scalars, query, out_grad, payloads[0], query_up_factor, value_up_factor,
            cos, sin, reach[None, :], window, lorad, held, lifts, first, count,
        )
        held, lifts = list(results[:4]), list(results[4:])
        first += count
    attended, key_mine, key_other, heads = held
    lift_q, lift_mine, lift_other = lifts
    lift_twin, key_other = lax.optimization_barrier((twin(lift_other), key_other))
    lifts = lift_mine + lift_twin.astype(F32)
    lift_near, lift_far = ahead(lifts[1].astype(BF), -1), ahead(lifts[2].astype(BF), -2)
    keyed = key_mine.astype(F32) + twin(key_other).astype(F32)
    own, one, two = keyed[0], keyed[1].astype(BF), keyed[2].astype(BF)
    lift_near, lift_far, own, one, two = lax.optimization_barrier((lift_near, lift_far, own, one, two))
    key_near = ahead(one, -1)
    kept, given = gradients(core[None], lift_q, lifts[0], lift_near, lift_far, normed_input, heads)
    kept = (kept.astype(F32) + twin(given).astype(F32)).astype(BF)
    cores = [list(range(c, devices, 2)) for c in range(2)]
    spread = lax.all_to_all(kept, "ctx", 0, 0, axis_index_groups=cores, tiled=True)
    key_near, two = lax.optimization_barrier((key_near, two))
    key_far = ahead(two, -2)
    gathered = lax.all_to_all(sum_and_copy(spread), "ctx", 0, 0, axis_index_groups=cores, tiled=True)
    sums = finish(core[None], gathered, twin(gathered), TOK * devices, normed_input.shape[1])
    key_total = (own + (key_near.astype(F32) + key_far.astype(F32))).reshape(TOK, HEADS, HD)
    swapped = jnp.concatenate([key_total[..., half:], key_total[..., :half]], axis=-1)
    key_grad = (key_total * cos[:, None, :] - swapped * sin[:, None, :]).astype(BF).reshape(TOK, HEADS * HD)
    down_q, up_q, down_v, up_v = sums
    return (attended, key_grad, down_q.T, up_q, down_v.T, up_v)


def solution(mesh):
    row = P("ctx", None)
    return jax.shard_map(
        on_device,
        mesh=mesh,
        in_specs=(row, row, row, row, row, P(), P(), P(), P(), P(), P()),
        out_specs=(row, row, P(), P(), P(), P()),
        check_vma=False,
    )
```

```python
import functools

import jax
import jax.numpy as jnp
from jax import lax
from jax.experimental import pallas as pl
from jax.experimental.pallas import tpu as pltpu
from jax.sharding import PartitionSpec as P

HD = 128
RANK = 64
TOK = 256
SUB = 128
REACH = 1152
SPANK = 5 * TOK
ROWS = 7 * TOK
KP = REACH
HEADS = 8
SHARE = 5
COUNTS = (3, 5)
UNIT = SHARE + 1
EDGE = UNIT * HEADS
VMEM_ASK = 60 * 2**20
THETA = 1000000.0
ADAPTER_SCALE = 2.0
LOG2E = 1.4426950408889634
NEG = -1e30
BF = jnp.bfloat16
F32 = jnp.float32


def mm(a, b):
    return lax.dot_general(a, b, (((1,), (0,)), ((), ())), preferred_element_type=F32)


def mm_nt(a, b):
    return lax.dot_general(a, b, (((1,), (1,)), ((), ())), preferred_element_type=F32)


def mm_tn(a, b):
    return lax.dot_general(a, b, (((0,), (0,)), ((), ())), preferred_element_type=F32)


def attention_kernel(share, first_call, sc, query, og, lora, qup, vup, cos, sin, dst, *rest):
    kin, vin, lin = rest[0:6], rest[6:12], rest[12:18]
    before_q, before_v = (None, None) if first_call else rest[18:20]
    rest = rest[18:] if first_call else rest[24:]
    att, dkm, dko, terms, liftq, lifts = rest[0:6]
    lvo = None if first_call else rest[6]
    rest = rest[6:] if first_call else rest[7:]
    kx, vx, kt, vt, lt, bias, ss, dka, dva, qn, dn, dnt, dqn, lva = rest
    g = pl.program_id(0)
    groups = pl.num_programs(0)
    wide = share * SUB
    scale = HD ** (-0.5)
    cexp = scale * LOG2E
    shift = pl.multiple_of(sc[0], TOK)

    def place(target, refs):
        for chip in range(3):
            low = pl.multiple_of((2 - chip) * 2 * TOK + shift, TOK)
            mine, other = refs[2 * chip], refs[2 * chip + 1]

            @pl.when(sc[1 + chip] == 0)
            def _():
                target[pl.ds(low, TOK), :] = mine[...]
                target[pl.ds(low + TOK, TOK), :] = other[...]

            @pl.when(sc[1 + chip] != 0)
            def _():
                target[pl.ds(low, TOK), :] = other[...]
                target[pl.ds(low + TOK, TOK), :] = mine[...]

    def take(read, mine, other):
        for chip in range(3):
            low = pl.multiple_of((2 - chip) * 2 * TOK + shift, TOK)

            @pl.when(sc[1 + chip] == 0)
            def _():
                mine[chip] = read(pl.ds(low, TOK)).astype(mine.dtype)
                other[chip] = read(pl.ds(low + TOK, TOK)).astype(other.dtype)

            @pl.when(sc[1 + chip] != 0)
            def _():
                mine[chip] = read(pl.ds(low + TOK, TOK)).astype(mine.dtype)
                other[chip] = read(pl.ds(low, TOK)).astype(other.dtype)

    @pl.when(g == 0)
    def _():
        for piece in (slice(0, TOK), slice(TOK + SPANK, ROWS)):
            dka[piece, :] = jnp.zeros((TOK, HD), F32)
            dva[piece, :] = jnp.zeros((TOK, HD), F32)
        if first_call:
            lva[...] = jnp.zeros_like(lva)
            liftq[...] = jnp.zeros_like(liftq)
        else:
            lva[...] = before_v[...]
            liftq[...] = before_q[...]
        place(kx, lin)
        lt[...] = kx[TOK : TOK + SPANK, :].T
        for b in range(2):
            first = dst[0:1, b * SUB : (b + 1) * SUB]
            last = SPANK - 2 * SUB + b * SUB + lax.broadcasted_iota(jnp.int32, (1, SUB), 1)
            key_at = b * SUB + lax.broadcasted_iota(jnp.int32, (REACH, SUB), 0)
            bias[b] = jnp.where((key_at >= first) & (key_at <= last), 0.0, NEG)

    place(kx, kin)
    place(vx, vin)
    kt[...] = kx[TOK : TOK + SPANK, :].T
    vt[...] = vx[TOK : TOK + SPANK, :].T
    for h in range(share):
        col = slice(h * HD, (h + 1) * HD)
        for b in range(2):
            qn[b, h * SUB : (h + 1) * SUB, :] = query[b * SUB : (b + 1) * SUB, col]
            dn[b, h * SUB : (h + 1) * SUB, :] = og[b * SUB : (b + 1) * SUB, col]
    pieces = [slice(i, i + KP) for i in range(0, REACH, KP)]

    keep = {}

    def phase_a(b):
        dnt[b] = dn[b].astype(F32).T
        query_t = qn[b].astype(F32).T.astype(BF)
        at = TOK + b * SUB
        top = None
        for piece in pieces:
            s = mm(kx[at + piece.start : at + piece.stop, :], query_t)
            s = s * cexp + jnp.concatenate([bias[b, piece, :]] * share, axis=1)
            ss[b, piece, :] = s
            t = jnp.max(s.reshape(KP // 8, 8, wide), axis=0)
            top = t if top is None else jnp.maximum(top, t)
        keep["top", b] = jnp.max(top, axis=0, keepdims=True)

    def phase_b(b):
        total = None
        for piece in pieces:
            e = jnp.exp2(ss[b, piece, :] - keep["top", b])
            t = jnp.sum(e.reshape(KP // 8, 8, wide), axis=0)
            total = t if total is None else total + t
        keep["norm", b] = keep["top", b] + jnp.log2(jnp.sum(total, axis=0, keepdims=True))

    def add(target, b, piece, value):
        rows = slice(TOK + b * SUB + piece.start, TOK + b * SUB + piece.stop)
        if b == 0:
            target[rows, :] = value
        elif piece.stop < REACH:
            target[rows, :] += value
        else:
            cut = KP - SUB
            target[rows.start : rows.start + cut, :] += value[:cut]
            target[rows.start + cut : rows.stop, :] = value[cut:]

    def phase_c(b):
        ot = None
        for piece in pieces:
            pb = jnp.exp2(ss[b, piece, :] - keep["norm", b]).astype(BF)
            t = mm(vt[:, b * SUB + piece.start : b * SUB + piece.stop], pb)
            ot = t if ot is None else ot + t
            add(dva, b, piece, mm(pb, dn[b]))
        ob = ot.astype(BF).astype(F32)
        keep["dot", b] = jnp.sum(dnt[b] * ob, axis=0, keepdims=True)
        obn = ob.T.astype(BF)
        for h in range(share):
            att[b * SUB : (b + 1) * SUB, h * HD : (h + 1) * HD] = obn[h * SUB : (h + 1) * SUB]

    def phase_d(b):
        qt = None
        grad_t = dnt[b].astype(BF)
        for piece in pieces:
            rows = slice(TOK + b * SUB + piece.start, TOK + b * SUB + piece.stop)
            p = jnp.exp2(ss[b, piece, :] - keep["norm", b])
            ds = (p * (mm(vx[rows, :], grad_t) - keep["dot", b])).astype(BF)
            t = mm(kt[:, b * SUB + piece.start : b * SUB + piece.stop], ds)
            qt = t if qt is None else qt + t
            add(dka, b, piece, mm(ds, qn[b]))
        dq = qt.T * scale
        rows = slice(b * SUB, (b + 1) * SUB)
        for h in range(share):
            u = dq[h * SUB : (h + 1) * SUB]
            dqn[rows, h * HD : (h + 1) * HD] = (
                u * cos[rows, :] - pltpu.roll(u, HD // 2, 1) * sin[rows, :]
            ).astype(BF)

    phase_a(0)
    phase_b(0)
    phase_a(1)
    phase_c(0)
    phase_b(1)
    phase_d(0)
    phase_c(1)
    phase_d(1)

    dqb = dqn[...]
    liftq[...] += mm_nt(dqb, qup[...])
    lora_t = lora[...].astype(F32).T[0:RANK].astype(BF)
    up = mm(lora_t, dqb)
    for h in range(share):
        terms[h] = (ADAPTER_SCALE * up[:, h * HD : (h + 1) * HD]).astype(BF)
    dvb = dva[TOK : TOK + SPANK, :].astype(BF)
    lva[TOK : TOK + SPANK, :] += mm_nt(dvb, vup[...])
    terms[share] = (ADAPTER_SCALE * mm(lt[...], dvb)[RANK : 2 * RANK]).astype(BF)
    take(lambda rows: (dka[rows, :] * scale).astype(BF), dkm, dko)

    @pl.when(g == groups - 1)
    def _():
        if first_call:
            lifts[...] = lva[...]
        else:
            take(lambda rows: lva[rows, :], lifts, lvo)


def prepare_kernel(normed, qdown, vdown, keys, values, vup, cos, sin, *outs):
    lora = mm_nt(normed[...], jnp.concatenate([qdown[...], vdown[...]], axis=0)).astype(BF)
    lora_v = lora[:, RANK:]
    head = 0
    for place, count in enumerate(COUNTS):
        out = outs[place]
        for c in range(count):
            col = slice((head + c) * HD, (head + c + 1) * HD)
            k = keys[:, col].astype(F32)
            k = k * cos[...] + pltpu.roll(k, HD // 2, 1) * sin[...]
            out[:, c * HD : (c + 1) * HD] = k.astype(BF)
            v = values[:, col].astype(F32) + ADAPTER_SCALE * mm(lora_v, vup[:, col])
            out[:, (count + c) * HD : (count + c + 1) * HD] = v.astype(BF)
        if place == 0:
            out[:, 2 * count * HD : (2 * count + 1) * HD] = lora
        head += count


def prepare(*operands):
    vmem = pl.BlockSpec(memory_space=pltpu.VMEM)
    widths = [2 * count * HD + (HD if place == 0 else 0) for place, count in enumerate(COUNTS)]
    return pl.pallas_call(
        prepare_kernel,
        out_shape=[jax.ShapeDtypeStruct((TOK, width), BF) for width in widths],
        in_specs=[vmem] * len(operands),
        out_specs=[vmem] * len(widths),
        compiler_params=pltpu.CompilerParams(vmem_limit_bytes=VMEM_ASK),
        name="prepare",
    )(*operands)


def rotate_kernel(frozen, lora, qup, cos, sin, query):
    extra = mm(lora[:, 0:RANK], qup[...])
    for h in range(SHARE):
        col = slice(h * HD, (h + 1) * HD)
        u = frozen[:, col].astype(F32) + ADAPTER_SCALE * extra[:, col]
        query[:, col] = (u * cos[...] + pltpu.roll(u, HD // 2, 1) * sin[...]).astype(BF)


def rotate_queries(frozen, own, qup, cos, sin):
    wide = SHARE * HD
    tail = 2 * COUNTS[0]
    table = pl.BlockSpec((TOK, HD), lambda g: (0, 0))
    return pl.pallas_call(
        rotate_kernel,
        out_shape=jax.ShapeDtypeStruct(frozen.shape, BF),
        grid=(HEADS,),
        in_specs=[
            pl.BlockSpec((TOK, wide), lambda g: (0, g)), pl.BlockSpec((TOK, HD), lambda g: (0, tail)),
            pl.BlockSpec((RANK, wide), lambda g: (0, g)), table, table,
        ],
        out_specs=pl.BlockSpec((TOK, wide), lambda g: (0, g)),
        compiler_params=pltpu.CompilerParams(vmem_limit_bytes=VMEM_ASK),
        name="rotate_queries",
    )(frozen, own, qup, cos, sin)


def gradients_kernel(core, total_q, own, near, far, normed, heads, kept, given):
    lift_q = (ADAPTER_SCALE * total_q[...]).astype(BF)
    lift_v = own[...] + (near[...].astype(F32) + far[...].astype(F32))
    lift_v = (ADAPTER_SCALE * lift_v).astype(BF)
    down = mm_tn(jnp.concatenate([lift_q, lift_v], axis=1), normed[...]).astype(BF)
    tiles = down.shape[1] // HD

    def write(low, high):
        for place, out in enumerate((low, high)):
            out[0 : EDGE // 2] = heads[place * EDGE // 2 : (place + 1) * EDGE // 2]
            for i in range(tiles // 2):
                col = slice((place * tiles // 2 + i) * HD, (place * tiles // 2 + i + 1) * HD)
                out[EDGE // 2 + i] = down[:RANK, col]
                out[EDGE // 2 + tiles // 2 + i] = down[RANK:, col]

    @pl.when(core[0] == 0)
    def _():
        write(kept, given)

    @pl.when(core[0] != 0)
    def _():
        write(given, kept)


def gradients(core, total_q, own, near, far, normed, heads):
    vmem = pl.BlockSpec(memory_space=pltpu.VMEM)
    half = jax.ShapeDtypeStruct((EDGE // 2 + normed.shape[1] // HD, RANK, HD), BF)
    return pl.pallas_call(
        gradients_kernel,
        out_shape=[half, half],
        in_specs=[pl.BlockSpec(memory_space=pltpu.SMEM)] + [vmem] * 6,
        out_specs=[vmem] * 2,
        compiler_params=pltpu.CompilerParams(vmem_limit_bytes=24 * 2**20),
        name="gradients",
    )(core, total_q, own, near, far, normed, heads)


def sum_kernel(spread, out):
    total = jnp.zeros(out.shape[1:], F32)
    for i in range(spread.shape[0]):
        total = total + spread[i].astype(F32)
    low = total.astype(BF)
    for i in range(spread.shape[0]):
        out[i] = low


def sum_and_copy(spread):
    vmem = pl.BlockSpec(memory_space=pltpu.VMEM)
    return pl.pallas_call(
        sum_kernel, out_shape=jax.ShapeDtypeStruct(spread.shape, BF), in_specs=[vmem], out_specs=vmem, name="sum_and_copy"
    )(spread)


def finish_kernel(scale, core, mine, other, down_q, up_q, down_v, up_v):
    def write(half):
        for i in range(HEADS // 2):
            for c in range(SHARE):
                at = (i * SHARE + c) * HD
                up_q[:, at : at + HD] = half[i * UNIT + c].astype(F32) * scale
            up_v[:, i * HD : (i + 1) * HD] = half[i * UNIT + SHARE].astype(F32) * scale
        tiles = down_q.shape[1] // HD
        for i in range(tiles):
            col = slice(i * HD, (i + 1) * HD)
            down_q[:, col] = half[EDGE // 2 + i].astype(F32) * scale
            down_v[:, col] = half[EDGE // 2 + tiles + i].astype(F32) * scale

    place = pl.program_id(0)

    @pl.when(core[0] == place)
    def _():
        write(mine)

    @pl.when(core[0] != place)
    def _():
        write(other)


def finish(core, mine, other, tokens, width):
    whole = pl.BlockSpec(mine.shape, lambda p: (0, 0, 0))
    shapes = [(RANK, width), (RANK, HEADS * SHARE * HD), (RANK, width), (RANK, HEADS * HD)]
    return pl.pallas_call(
        functools.partial(finish_kernel, 1.0 / tokens),
        out_shape=[jax.ShapeDtypeStruct(shape, F32) for shape in shapes],
        grid=(2,),
        in_specs=[pl.BlockSpec(memory_space=pltpu.SMEM), whole, whole],
        out_specs=[pl.BlockSpec((shape[0], shape[1] // 2), lambda p: (0, p)) for shape in shapes],
        compiler_params=pltpu.CompilerParams(vmem_limit_bytes=VMEM_ASK),
        name="finish",
    )(core, mine, other)


def attention(scalars, query, grad, own, qup, vup, cos, sin, dst, keyed, lorad, held, lifts, first, count):
    share = SHARE
    wide = share * HD
    tail = 2 * COUNTS[0]

    def whole(shape):
        return pl.BlockSpec(shape, lambda g, s: (0,) * len(shape))

    def column(rows, width, offset):
        return pl.BlockSpec((rows, width), lambda g, s: (0, g + offset))

    lora_spec = pl.BlockSpec((TOK, HD), lambda g, s: (0, tail))
    in_specs = [
        column(TOK, wide, first), column(TOK, wide, first), lora_spec,
        column(RANK, wide, first), column(RANK, HD, first),
        whole((TOK, HD)), whole((TOK, HD)), whole((1, TOK)),
    ]
    in_specs += [column(TOK, HD, 0)] * 6 + [column(TOK, HD, count)] * 6 + [lora_spec] * 6
    operands = [scalars, query, grad, own, qup, vup, cos, sin, dst, *keyed, *keyed, *lorad]
    aliases = {}
    if held is not None:
        operands += lifts
        in_specs += [whole((TOK, RANK)), whole((ROWS, RANK))]
        aliases = {len(operands) + i: i for i in range(len(held))}
        operands += held
        in_specs += [pl.BlockSpec(memory_space=pl.ANY)] * len(held)
    pair = jax.ShapeDtypeStruct((3, TOK, HEADS * HD), BF)
    lift = (3, TOK, RANK)
    out_shape = [
        jax.ShapeDtypeStruct(query.shape, BF), pair, pair, jax.ShapeDtypeStruct((EDGE, RANK, HD), BF),
        jax.ShapeDtypeStruct((TOK, RANK), F32),
    ]
    if held is None:
        out_shape += [jax.ShapeDtypeStruct((ROWS, RANK), F32)]
        lift_specs = [whole((ROWS, RANK))]
    else:
        out_shape += [jax.ShapeDtypeStruct(lift, F32), jax.ShapeDtypeStruct(lift, BF)]
        lift_specs = [whole(lift)] * 2
    pair_spec = pl.BlockSpec((3, TOK, HD), lambda g, s: (0, 0, g + first))
    out_specs = [
        column(TOK, wide, first), pair_spec, pair_spec,
        pl.BlockSpec((UNIT, RANK, HD), lambda g, s: (g + first, 0, 0)),
        whole((TOK, RANK)), *lift_specs,
    ]
    wide_rows = share * SUB
    scratch = [
        pltpu.VMEM((ROWS, HD), BF), pltpu.VMEM((ROWS, HD), BF),
        pltpu.VMEM((HD, SPANK), BF), pltpu.VMEM((HD, SPANK), BF), pltpu.VMEM((HD, SPANK), BF),
        pltpu.VMEM((2, REACH, SUB), F32),
        pltpu.VMEM((2, REACH, wide_rows), F32),
        pltpu.VMEM((ROWS, HD), F32), pltpu.VMEM((ROWS, HD), F32),
        pltpu.VMEM((2, wide_rows, HD), BF), pltpu.VMEM((2, wide_rows, HD), BF),
        pltpu.VMEM((2, HD, wide_rows), F32), pltpu.VMEM((TOK, wide), BF),
        pltpu.VMEM((ROWS, RANK), F32),
    ]
    return pl.pallas_call(
        functools.partial(attention_kernel, share, held is None),
        out_shape=out_shape,
        grid_spec=pltpu.PrefetchScalarGridSpec(
            num_scalar_prefetch=1, grid=(count,), in_specs=in_specs, out_specs=out_specs, scratch_shapes=scratch
        ),
        input_output_aliases=aliases,
        compiler_params=pltpu.CompilerParams(
            dimension_semantics=("arbitrary",), vmem_limit_bytes=VMEM_ASK
        ),
        cost_estimate=pl.CostEstimate(
            flops=12 * 2 * REACH * SUB * share * HD * count, transcendentals=2 * REACH * SUB * share * count,
            bytes_accessed=6 * 2**20 * count // HEADS,
        ),
        name="attention",
    )(*operands)


def moved(block, step):
    devices = range(lax.axis_size("ctx"))
    route = [(i, step(i)) for i in devices if step(i) in devices]
    return lax.ppermute(block, "ctx", route)


def twin(block):
    return moved(block, lambda i: i ^ 1)


def ahead(block, chips):
    return moved(block, lambda i: i + 2 * chips)


def on_device(
    normed_input,
    frozen_query_output,
    key_base,
    frozen_value_output,
    out_grad,
    query_down_factor,
    query_up_factor,
    value_down_factor,
    value_up_factor,
    doc_lengths,
    stretch_map,
):
    devices = lax.axis_size("ctx")
    mine = lax.axis_index("ctx")
    chip, core = mine // 2, mine % 2
    stretch = stretch_map[mine]
    steps = jnp.arange(TOK, dtype=jnp.int32)
    places = stretch * TOK + steps
    documents = jnp.arange(doc_lengths.shape[0], dtype=jnp.int32)
    ends = jnp.sum(jnp.where(documents[:, None] >= documents[None, :], doc_lengths[None, :], 0), axis=1)
    starts = jnp.max(jnp.where(ends[None, :] <= places[:, None], ends[None, :], 0), axis=1)
    local = places - starts
    reach = 4 * TOK + steps - local
    half = HD // 2
    inverse = THETA ** (-jnp.arange(half, dtype=F32) * 2.0 / HD)
    angles = local.astype(F32)[:, None] * inverse[None, :]
    cosine, sine = jnp.cos(angles), jnp.sin(angles)
    cos = jnp.concatenate([cosine, cosine], axis=1)
    sin = jnp.concatenate([-sine, sine], axis=1)
    chips = chip - jnp.arange(3, dtype=jnp.int32)
    flips = (core + stretch_map[2 * jnp.maximum(chips, 0)]) % 2
    scalars = jnp.concatenate([(TOK * (1 - stretch % 2))[None], flips]).astype(jnp.int32)

    payloads = prepare(
        normed_input, query_down_factor.T, value_down_factor.T, key_base, frozen_value_output, value_up_factor, cos, sin
    )
    twins = [twin(payload) for payload in payloads]
    near = [ahead(payload, 1) for payload in payloads]
    far = [ahead(payload, 2) for payload in payloads]
    query = rotate_queries(frozen_query_output, payloads[0], query_up_factor, cos, sin)
    near[0], far[0], query = lax.optimization_barrier((near[0], far[0], query))
    lorad = held = lifts = None
    first = 0
    for place, count in enumerate(COUNTS):
        one, two = near[place], far[place]
        if held is not None:
            one, two, held[0] = lax.optimization_barrier((one, two, held[0]))
        window = [payloads[place], twins[place], one, twin(one), two, twin(two)]
        lorad = window if lorad is None else lorad
        results = attention(
            scalars, query, out_grad, payloads[0], query_up_factor, value_up_factor,
            cos, sin, reach[None, :], window, lorad, held, lifts, first, count,
        )
        held, lifts = list(results[:4]), list(results[4:])
        first += count
    attended, key_mine, key_other, heads = held
    lift_q, lift_mine, lift_other = lifts
    lift_twin, key_other = lax.optimization_barrier((twin(lift_other), key_other))
    lifts = lift_mine + lift_twin.astype(F32)
    lift_near, lift_far = ahead(lifts[1].astype(BF), -1), ahead(lifts[2].astype(BF), -2)
    keyed = key_mine.astype(F32) + twin(key_other).astype(F32)
    own, one, two = keyed[0], keyed[1].astype(BF), keyed[2].astype(BF)
    lift_near, lift_far, own, one, two = lax.optimization_barrier((lift_near, lift_far, own, one, two))
    key_far = ahead(two, -2)
    kept, given = gradients(core[None], lift_q, lifts[0], lift_near, lift_far, normed_input, heads)
    kept = (kept.astype(F32) + twin(given).astype(F32)).astype(BF)
    cores = [list(range(c, devices, 2)) for c in range(2)]
    spread = lax.all_to_all(kept, "ctx", 0, 0, axis_index_groups=cores, tiled=True)
    key_far, one = lax.optimization_barrier((key_far, one))
    key_near = ahead(one, -1)
    gathered = lax.all_to_all(sum_and_copy(spread), "ctx", 0, 0, axis_index_groups=cores, tiled=True)
    sums = finish(core[None], gathered, twin(gathered), TOK * devices, normed_input.shape[1])
    key_total = (own + (key_near.astype(F32) + key_far.astype(F32))).reshape(TOK, HEADS, HD)
    swapped = jnp.concatenate([key_total[..., half:], key_total[..., :half]], axis=-1)
    key_grad = (key_total * cos[:, None, :] - swapped * sin[:, None, :]).astype(BF).reshape(TOK, HEADS * HD)
    down_q, up_q, down_v, up_v = sums
    return (attended, key_grad, down_q.T, up_q, down_v.T, up_v)


def solution(mesh):
    row = P("ctx", None)
    return jax.shard_map(
        on_device,
        mesh=mesh,
        in_specs=(row, row, row, row, row, P(), P(), P(), P(), P(), P()),
        out_specs=(row, row, P(), P(), P(), P()),
        check_vma=False,
    )
```
